32 devices in a mesh: prow: 8 (over z, y), pcol: 4 (over x, core).
Axes of the slice: x: 2, y: 2, z: 4, core: 2. Of those that a mesh axis runs over, the one named last changes fastest.
Arguments:
- inverse_tiles: bfloat16 [24576, 24576], P('prow', 'pcol'), may hold values from -6 to 6
- panel_blocks: bfloat16 [24576, 1536], P(('prow', 'pcol')), may hold values from -0.0546875 to 0.0546875
- pivot_inverse: bfloat16 [3, 512, 512], replicated, may hold values from -0.25 to 0.25
- diagonal_inverse: float32 [3, 512, 512], replicated, may hold values from -6 to 6
- ancestors: int32 [3, 24], replicated, may hold values from 0 to 47, all different within a row
Outputs:
- cross_blocks: float32 [24576, 1536], P(('prow', 'pcol'))
- diagonal_blocks: float32 [3, 512, 512], replicated
The draws below stay inside these ranges and needn't reach their ends.
Inputs may be any that keep to these rules, and one draw needn't show every extreme that they name: `ancestors`: each row names 24 different blocks, and every block is named by some row.
All inputs are finite; a program needn't handle non-finite values.
Results may differ from the reference program's by a relative error of at most 0.003.
Values may be sent and summed in bfloat16 or wider, within the bound.
A program may use at most 128 MiB of HBM per device.

```python
import jax
import jax.numpy as jnp
from jax import lax

WIDTH = 512
BLOCKS = 48
LISTED = 24
SUPERNODES = 3
ORDER = 24576


def shard_levels(rng, extent, shards, smallest, high):
    loudness = 1.0
    for axis_at, blocks in shards:
        draws = jax.random.uniform(jax.random.fold_in(jax.random.fold_in(rng, 6), axis_at), (blocks,), jnp.float32, smallest / len(shards), high / len(shards))
        loudness = loudness * jnp.repeat(jnp.exp(draws), extent[axis_at] // blocks).reshape((-1,) + (1,) * (len(extent) - 1 - axis_at))
    return loudness


def distinct(rng, rows, count, top, lift):
    sequence = jax.random.permutation(jax.random.fold_in(rng, 1), count)
    pull = sequence
    for power in range(3):
        pull = pull * pull // count
    pull = pull * lift // count
    chance = jax.random.randint(jax.random.fold_in(rng, 2), (rows, count), 0, 4096) + pull
    sure = jax.random.permutation(jax.random.fold_in(rng, 3), rows)[jnp.arange(count) % rows]
    chance = jnp.where(jnp.arange(rows)[:, None] == sure[None, :], 1 << 14, chance)
    score = chance * count + jnp.arange(count)
    return lax.top_k(score.astype(jnp.int32), top)[1].astype(jnp.int32)


def centred(own_key, extent, width, most, shards=(), kind=jnp.bfloat16):
    array = jax.random.normal(own_key, extent, jnp.float32) * width
    if len(shards) > 0:
        array = shard_levels(own_key, extent, shards, -0.22, 0.18) * array
    return jnp.clip(array, min=-most, max=most).astype(kind)


def setup_inputs(seed: int = 0) -> dict:
    keys = jax.random.split(jax.random.key(seed), 6)
    inverse_tiles = centred(keys[0], (ORDER, ORDER), 1.0, 6.0, ((0, 8), (1, 4)))
    panel_blocks = centred(keys[1], (ORDER, SUPERNODES * WIDTH), (LISTED * WIDTH) ** -0.5, 0.0546875, ((0, 32),))
    pivot_inverse = centred(keys[2], (SUPERNODES, WIDTH, WIDTH), WIDTH ** -0.5, 0.25)
    diagonal_inverse = centred(keys[3], (SUPERNODES, WIDTH, WIDTH), 1.0, 6.0, (), jnp.float32)
    ancestors = distinct(keys[4], SUPERNODES, BLOCKS, LISTED, 4096)
    return {"inverse_tiles": inverse_tiles, "panel_blocks": panel_blocks, "pivot_inverse": pivot_inverse, "diagonal_inverse": diagonal_inverse, "ancestors": ancestors}


def reference(inverse_tiles, panel_blocks, pivot_inverse, diagonal_inverse, ancestors):
    rows_all = BLOCKS * WIDTH
    member = jnp.any(ancestors[:, :, None] == jnp.arange(BLOCKS, dtype=jnp.int32)[None, None, :], axis=1).astype(jnp.float32)
    listed = jnp.repeat(member.T, WIDTH, axis=0)
    raw_three = panel_blocks.reshape(rows_all, SUPERNODES, WIDTH).astype(jnp.float32)
    normed = jnp.einsum("rsw,swv->rsv", raw_three, pivot_inverse.astype(jnp.float32), precision=lax.Precision.HIGHEST)
    scaled = (normed * listed[:, :, None]).astype(jnp.bfloat16)
    panel = scaled.reshape(rows_all, SUPERNODES * WIDTH)

    def one_block(tile_rows):
        return jnp.dot(tile_rows, panel, preferred_element_type=jnp.float32)

    product = lax.map(one_block, inverse_tiles.reshape(BLOCKS, WIDTH, rows_all))
    product = product.reshape(rows_all, SUPERNODES, WIDTH)
    cross = -(product * listed[:, :, None])
    terms = jnp.einsum("rsw,rsv->swv", scaled.astype(jnp.float32), cross, precision=lax.Precision.HIGHEST)
    diagonal = diagonal_inverse - terms
    return cross.reshape(rows_all, SUPERNODES * WIDTH), diagonal
```

```python
import functools
import math

import jax
import jax.numpy as jnp
from jax import lax
from jax.experimental import pallas as pl
from jax.experimental.pallas import tpu as pltpu
from jax.sharding import PartitionSpec as P

MESH = pl.DeviceIdType.MESH
DEPTH = 6


def reduce_rows(partial, seg_rows):
    devices = lax.axis_size("pcol")
    width = partial.shape[1]
    me = lax.axis_index("pcol")
    if devices & (devices - 1):
        return lax.psum_scatter(partial, "pcol", scatter_dimension=0, tiled=True)
    value = partial.reshape(devices, seg_rows, width)
    bit = 1
    while bit < devices:
        mine = (me // bit) % 2
        halves = value.reshape(value.shape[0] // 2, 2, seg_rows, width)
        keep = jnp.where(mine == 0, halves[:, 0], halves[:, 1])
        send = jnp.where(mine == 0, halves[:, 1], halves[:, 0]).astype(jnp.bfloat16)
        got = lax.ppermute(send, "pcol", [(d, d ^ bit) for d in range(devices)])
        value = keep + got.astype(jnp.float32)
        bit *= 2
    return value.reshape(seg_rows, width)


def sum_everywhere(terms):
    axes = ("prow", "pcol")
    devices = lax.axis_size("prow") * lax.axis_size("pcol")
    rows = terms.shape[0] * terms.shape[1]
    if devices & (devices - 1) or rows % devices:
        return lax.psum(terms, axes)
    me = lax.axis_index("prow") * lax.axis_size("pcol") + lax.axis_index("pcol")
    value = terms.reshape(rows, terms.shape[2])
    bits = []
    bit = 1
    while bit < devices:
        bits.append(bit)
        bit *= 2
    for bit in bits:
        low = (me // bit) % 2 == 0
        half = value.shape[0] // 2
        keep = jnp.where(low, value[:half], value[half:])
        send = jnp.where(low, value[half:], value[:half])
        value = keep + lax.ppermute(send, axes, [(d, d ^ bit) for d in range(devices)])
    value = value.astype(jnp.bfloat16)
    for bit in reversed(bits):
        low = (me // bit) % 2 == 0
        got = lax.ppermute(value, axes, [(d, d ^ bit) for d in range(devices)])
        value = jnp.concatenate(
            [jnp.where(low, value, got), jnp.where(low, got, value)], axis=0
        )
    return value.astype(jnp.float32).reshape(terms.shape)


def general(inverse_tiles, panel_blocks, pivot_inverse, diagonal_inverse, ancestors):
    seg_rows = panel_blocks.shape[0]
    n_super = pivot_inverse.shape[0]
    width = pivot_inverse.shape[1]
    row_devices = lax.axis_size("prow")
    col_devices = lax.axis_size("pcol")
    segment = lax.axis_index("prow") * col_devices + lax.axis_index("pcol")
    row_ids = segment * seg_rows + lax.iota(jnp.int32, seg_rows)
    block_ids = row_ids // width
    listed = jnp.any(block_ids[:, None, None] == ancestors[None, :, :], axis=2).astype(jnp.float32)
    route = []
    for s in range(row_devices * col_devices):
        route.append((s, (s % row_devices) * col_devices + s // row_devices))
    crosses, terms, panels, scaled = [], [], [], []
    for k in range(n_super):
        normed = jnp.dot(
            panel_blocks[:, k * width:(k + 1) * width], pivot_inverse[k],
            preferred_element_type=jnp.float32,
        )
        own = (normed * listed[:, k:k + 1]).astype(jnp.bfloat16)
        scaled.append(own)
        moved = lax.ppermute(own, ("prow", "pcol"), route)
        panels.append(lax.all_gather(moved, "prow", axis=0, tiled=True))
    for k in range(n_super):
        product = jnp.dot(inverse_tiles, panels[k], preferred_element_type=jnp.float32)
        cross = -(reduce_rows(product, seg_rows) * listed[:, k:k + 1])
        crosses.append(cross)
        terms.append(lax.dot_general(
            scaled[k].astype(jnp.float32), cross, (((0,), (0,)), ((), ())),
            precision=lax.Precision.HIGHEST,
        ))
    diagonal = diagonal_inverse - sum_everywhere(jnp.stack(terms))
    return (jnp.concatenate(crosses, axis=1), diagonal)


def remote(src, dst, send, recv, device):
    return pltpu.make_async_remote_copy(
        src_ref=src, dst_ref=dst, send_sem=send, recv_sem=recv,
        device_id=device, device_id_type=MESH,
    )


def gather_kernel(nz, ny, nc, n_super, chunk, steps, place, own, out, dense, lane,
                  s1, r1, su, sd, rz, sp, ro, sy):
    lanes = ny * nc
    per = own.shape[1]
    halves = lane.shape[2]
    p, c = lax.axis_index("prow"), lax.axis_index("pcol")
    z, y = p // ny, lax.rem(p, ny)
    e = y * nc + c

    def peer(o):
        other = lax.rem(e + o, lanes)
        return other, (z * ny + other // nc, lax.rem(other, nc))

    barrier = pltpu.get_barrier_semaphore()
    for o in range(1, lanes):
        pl.semaphore_signal(barrier, inc=1, device_id=peer(o)[1], device_id_type=MESH)

    @pl.when(z > 0)
    def _():
        pl.semaphore_signal(barrier, inc=1, device_id=(p - ny, c), device_id_type=MESH)

    @pl.when(z < nz - 1)
    def _():
        pl.semaphore_signal(barrier, inc=1, device_id=(p + ny, c), device_id_type=MESH)

    near = jnp.where(z > 0, 1, 0) + jnp.where(z < nz - 1, 1, 0)
    pl.semaphore_wait(barrier, lanes - 1 + near)

    def deal(o):
        other, device = peer(o)
        return remote(own.at[other], dense.at[pl.ds(e * per, per)], s1.at[o], r1.at[e], device)

    for o in range(1, lanes):
        deal(o).start()
    home = pltpu.make_async_copy(own.at[e], dense.at[pl.ds(e * per, per)], r1.at[e])
    home.start()
    home.wait()
    for o in range(1, lanes):
        other, device = peer(o)
        part = dense.at[pl.ds(other * per, per)]
        remote(part, part, s1.at[o], r1.at[other], device).wait_recv()

    def span(t):
        return pl.ds(t * chunk, chunk)

    def up(g, t):
        part = lane.at[g, span(t)]
        return remote(part, part, su.at[g, t], rz.at[g, t], (p + ny, c))

    def down(g, t):
        part = lane.at[g, span(t)]
        return remote(part, part, sd.at[g, t], rz.at[g, t], (p - ny, c))

    def cross_plane(g, t):
        return remote(lane.at[g, span(t)], out.at[span(t), :, e], sp.at[g, t], ro.at[e, t], (p, g))

    def stay(t):
        return pltpu.make_async_copy(lane.at[c, span(t)], out.at[span(t), :, e], sp.at[c, t])

    def across(l, o, t):
        part = out.at[span(t), :, y * nc + l]
        return remote(part, part, sy.at[l, o - 1, t], ro.at[y * nc + l, t],
                      (z * ny + lax.rem(y + o, ny), c))

    def arrived(other, t):
        part = out.at[span(t), :, other]
        remote(part, part, sp.at[0, t], ro.at[other, t], (p, c)).wait_recv()

    def spread(g, t):
        @pl.when(jnp.logical_and(g <= z, z < nz - 1))
        def _():
            up(g, t).start()

        @pl.when(jnp.logical_and(g >= z, z > 0))
        def _():
            down(g, t).start()

        @pl.when(g != c)
        def _():
            cross_plane(g, t).start()

        @pl.when(g == c)
        def _():
            stay(t).start()

    away = jnp.maximum(z - c, c - z)

    def step(tau, carry):
        @pl.when(tau < steps)
        def _():
            def pack(i, carry):
                s = tau * chunk + i
                at = place[s]
                for h in range(halves):
                    lane[z, s, h] = dense[at + h * n_super]
                return carry
            lax.fori_loop(0, chunk, pack, 0)
            spread(z, tau)

        for d in range(1, nz):
            t = tau - d
            live = jnp.logical_and(t >= 0, t < steps)
            for g, ok in ((z - d, z - d >= 0), (z + d, z + d < nz)):
                @pl.when(jnp.logical_and(live, ok))
                def _():
                    part = lane.at[g, span(t)]
                    remote(part, part, su.at[g, t], rz.at[g, t], (p, c)).wait_recv()
                    spread(g, t)

        t = tau - 1 - away

        @pl.when(jnp.logical_and(t >= 0, t < steps))
        def _():
            for l in range(nc):
                @pl.when(l == c)
                def _():
                    stay(t).wait()

                @pl.when(l != c)
                def _():
                    arrived(y * nc + l, t)

                for o in range(1, ny):
                    across(l, o, t).start()
        return carry

    lax.fori_loop(0, steps + nz, step, 0)

    def finish(t, carry):
        for o in range(1, ny):
            for l in range(nc):
                arrived(lax.rem(y + o, ny) * nc + l, t)
        for o in range(1, ny):
            for l in range(nc):
                across(l, o, t).wait_send()
        for g in range(nz):
            @pl.when(jnp.logical_and(g <= z, z < nz - 1))
            def _():
                up(g, t).wait_send()

            @pl.when(jnp.logical_and(g >= z, z > 0))
            def _():
                down(g, t).wait_send()

            @pl.when(g != c)
            def _():
                cross_plane(g, t).wait_send()
        return carry

    lax.fori_loop(0, steps, finish, 0)
    for o in range(1, lanes):
        deal(o).wait_send()


def multiply_kernel(table, meta, cover, tiles, recv, out, buf, held, asem, hsem):
    width = out.shape[1]
    depth = buf.shape[0]
    n, base, listed = meta[0], meta[1], meta[2]

    def fetch(i):
        rows = pl.ds(pl.multiple_of(table[0, i] * width, width), width)
        cols = pl.ds(pl.multiple_of(table[1, i] * width, width), width)
        at = lax.rem(i, depth)
        return pltpu.make_async_copy(tiles.at[rows, cols], buf.at[at], asem.at[at])

    def slot(j):
        return pltpu.make_async_copy(recv.at[base + j], held.at[j], hsem.at[j])

    def begin(j, carry):
        slot(j).start()

        @pl.when(j < jnp.minimum(n, depth - 1))
        def _():
            fetch(j).start()
        return carry

    lax.fori_loop(0, listed, begin, 0)

    def more(j, carry):
        @pl.when(j < n)
        def _():
            fetch(j).start()
        return carry

    lax.fori_loop(jnp.minimum(listed, depth - 1), depth - 1, more, 0)
    for r in range(out.shape[0]):
        @pl.when(cover[r] == 0)
        def _():
            out[r] = jnp.zeros(out.shape[1:], out.dtype)

    def item(i, carry):
        @pl.when(i + depth - 1 < n)
        def _():
            fetch(i + depth - 1).start()

        j = table[2, i]

        @pl.when(i < listed)
        def _():
            slot(j).wait()

        fetch(i).wait()
        product = jnp.dot(buf[lax.rem(i, depth)], held[j], preferred_element_type=jnp.float32)
        r = table[0, i]

        @pl.when(j == 0)
        def _():
            out[r] = product

        @pl.when(j > 0)
        def _():
            out[r] += product
        return carry

    lax.fori_loop(0, n, item, 0)

    @pl.when(n == 0)
    def _():
        def drop(j, carry):
            slot(j).wait()
            return carry
        lax.fori_loop(0, listed, drop, 0)


def squeeze(flags, size):
    flags = flags.astype(jnp.int32)
    where = jnp.arange(flags.shape[0])
    rank = jnp.sum(jnp.where(where[None, :] < where[:, None], flags[None, :], 0), axis=1)
    hit = jnp.logical_and(rank[None, :] == jnp.arange(size)[:, None], flags[None, :] > 0)
    index = jnp.sum(jnp.where(hit, where[None, :], 0), axis=1)
    return rank, index.astype(jnp.int32)


def compact(slots, chunk, collective_id, ny, member, inverse_tiles, panel_blocks, pivot_inverse,
            diagonal_inverse):
    seg_rows = panel_blocks.shape[0]
    n_super, width = pivot_inverse.shape[0], pivot_inverse.shape[1]
    nr, nc = lax.axis_size("prow"), lax.axis_size("pcol")
    nz, lanes = nr // ny, ny * nc
    p, c = lax.axis_index("prow"), lax.axis_index("pcol")
    z = p // ny
    row_blocks = inverse_tiles.shape[0] // width
    col_blocks = inverse_tiles.shape[1] // width
    sub = math.gcd(seg_rows, width)
    parts, halves, thin = seg_rows // sub, width // sub, sub // lanes

    segment = p * nc + c
    block_ids = (segment * seg_rows + lax.iota(jnp.int32, seg_rows)) // width
    listed = jnp.take(member, block_ids, axis=0).astype(jnp.float32)
    scaled = []
    for k in range(n_super):
        normed = jnp.dot(
            panel_blocks[:, k * width:(k + 1) * width], pivot_inverse[k],
            preferred_element_type=jnp.float32,
        )
        scaled.append((normed * listed[:, k:k + 1]).astype(jnp.bfloat16))
    own = jnp.stack([s.reshape(parts, lanes, thin, width) for s in scaled], axis=1)
    own = own.transpose(2, 0, 1, 3, 4).reshape(lanes, parts * n_super, thin, width)

    of_plane = lax.dynamic_slice_in_dim(member, z * col_blocks, col_blocks, 0).T.reshape(-1)
    _, index = squeeze(of_plane, slots)
    place = index % col_blocks * (halves * n_super) + index // col_blocks
    steps = slots // chunk
    sems = [
        (lanes,), (lanes,), (nz, steps), (nz, steps), (nz, steps), (nz, steps), (lanes, steps),
        (nc, max(ny - 1, 1), steps),
    ]
    recv = pl.pallas_call(
        functools.partial(gather_kernel, nz, ny, nc, n_super, chunk, steps),
        out_shape=jax.ShapeDtypeStruct((slots, halves, lanes, thin, width), jnp.bfloat16),
        in_specs=[pl.BlockSpec(memory_space=pltpu.SMEM), pl.BlockSpec(memory_space=pl.ANY)],
        out_specs=pl.BlockSpec(memory_space=pl.ANY),
        scratch_shapes=[
            pltpu.VMEM((lanes * parts * n_super, thin, width), jnp.bfloat16),
            pltpu.VMEM((nz, slots, halves, thin, width), jnp.bfloat16),
        ] + [pltpu.SemaphoreType.DMA(s) for s in sems],
        compiler_params=pltpu.CompilerParams(
            collective_id=collective_id, has_side_effects=True, vmem_limit_bytes=40 * 2**20,
        ),
        name="gather_listed",
    )(place, own)
    recv = recv.reshape(slots, width, width)

    of_cols = lax.dynamic_slice_in_dim(member, c * col_blocks, col_blocks, 0)
    of_rows = lax.dynamic_slice_in_dim(member, p * row_blocks, row_blocks, 0)
    counts = jnp.sum(of_cols.astype(jnp.int32), axis=0)
    crosses, terms = [], []
    for k in range(n_super):
        both = jnp.logical_and(of_rows[:, k:k + 1], of_cols[None, :, k]).reshape(-1)
        _, index = squeeze(both, both.shape[0])
        rank, _ = squeeze(of_cols[:, k], 1)
        r, j = index // col_blocks, index % col_blocks
        table = jnp.stack([r, j, jnp.take(rank, j)]).astype(jnp.int32)
        base = jnp.sum(counts[:k]) if k else jnp.int32(0)
        meta = jnp.stack([jnp.sum(both.astype(jnp.int32)), base, counts[k]]).astype(jnp.int32)
        cover = jnp.logical_and(of_rows[:, k], counts[k] > 0).astype(jnp.int32)
        product = pl.pallas_call(
            multiply_kernel,
            out_shape=jax.ShapeDtypeStruct((row_blocks, width, width), jnp.float32),
            in_specs=[pl.BlockSpec(memory_space=pltpu.SMEM)] * 3
            + [pl.BlockSpec(memory_space=pl.ANY)] * 2,
            out_specs=pl.BlockSpec(memory_space=pltpu.VMEM),
            scratch_shapes=[
                pltpu.VMEM((DEPTH, width, width), jnp.bfloat16),
                pltpu.VMEM((col_blocks, width, width), jnp.bfloat16),
                pltpu.SemaphoreType.DMA((DEPTH,)),
                pltpu.SemaphoreType.DMA((col_blocks,)),
            ],
            compiler_params=pltpu.CompilerParams(vmem_limit_bytes=40 * 2**20),
            cost_estimate=pl.CostEstimate(
                flops=row_blocks * col_blocks * width**3, bytes_accessed=2 * width * width * 40,
                transcendentals=0),
            name="multiply_listed",
        )(table, meta, cover, inverse_tiles, recv)
        summed = reduce_rows(product.reshape(row_blocks * width, width), seg_rows)
        cross = -(summed * listed[:, k:k + 1])
        crosses.append(cross)
        terms.append(lax.dot_general(
            scaled[k].astype(jnp.float32), cross, (((0,), (0,)), ((), ())),
            precision=lax.Precision.HIGHEST,
        ))
    diagonal = diagonal_inverse - sum_everywhere(jnp.stack(terms))
    return (jnp.concatenate(crosses, axis=1), diagonal)


def on_device(inverse_tiles, panel_blocks, pivot_inverse, diagonal_inverse, ancestors):
    arrays = (inverse_tiles, panel_blocks, pivot_inverse, diagonal_inverse)
    nr, nc = lax.axis_size("prow"), lax.axis_size("pcol")
    n_super, width = pivot_inverse.shape[0], pivot_inverse.shape[1]
    seg_rows = panel_blocks.shape[0]
    ny = nr // nc
    sub = math.gcd(seg_rows, width)
    fits = (
        nr == ny * nc and ny > 1 and sub % (ny * nc * 16) == 0
        and inverse_tiles.shape[0] % width == 0 and inverse_tiles.shape[1] % width == 0
    )
    if not fits:
        return general(*arrays, ancestors)
    blocks = nr * nc * seg_rows // width
    member = jnp.any(jnp.arange(blocks)[:, None, None] == ancestors[None, :, :], axis=2)
    every = blocks // nc * n_super
    sizes = [(every * 11 // 18, 2), (every, 4)]
    sizes = [(s - s % chunk, chunk) for s, chunk in sizes]
    largest = jnp.max(jnp.sum(member.reshape(nc, -1).astype(jnp.int32), axis=1))
    level = sum((largest > s).astype(jnp.int32) for s, _ in sizes[:-1])
    branches = [
        functools.partial(compact, s, chunk, i, ny) for i, (s, chunk) in enumerate(sizes)
    ]
    return lax.switch(level, branches, member, *arrays)


def solution(mesh):
    in_specs = (P("prow", "pcol"), P(("prow", "pcol"), None), P(), P(), P())
    out_specs = (P(("prow", "pcol"), None), P())
    return jax.shard_map(
        on_device, mesh=mesh, in_specs=in_specs, out_specs=out_specs, check_vma=False
    )
```

```python
import functools
import math

import jax
import jax.numpy as jnp
from jax import lax
from jax.experimental import pallas as pl
from jax.experimental.pallas import tpu as pltpu
from jax.sharding import PartitionSpec as P

MESH = pl.DeviceIdType.MESH
DEPTH = 6


def reduce_rows(partial, seg_rows):
    devices = lax.axis_size("pcol")
    width = partial.shape[1]
    me = lax.axis_index("pcol")
    if devices & (devices - 1):
        return lax.psum_scatter(partial, "pcol", scatter_dimension=0, tiled=True)
    value = partial.reshape(devices, seg_rows, width)
    bit = 1
    while bit < devices:
        mine = (me // bit) % 2
        halves = value.reshape(value.shape[0] // 2, 2, seg_rows, width)
        keep = jnp.where(mine == 0, halves[:, 0], halves[:, 1])
        send = jnp.where(mine == 0, halves[:, 1], halves[:, 0]).astype(jnp.bfloat16)
        got = lax.ppermute(send, "pcol", [(d, d ^ bit) for d in range(devices)])
        value = keep + got.astype(jnp.float32)
        bit *= 2
    return value.reshape(seg_rows, width)


def sum_everywhere(terms):
    axes = ("prow", "pcol")
    devices = lax.axis_size("prow") * lax.axis_size("pcol")
    rows = terms.shape[0] * terms.shape[1]
    if devices & (devices - 1) or rows % devices:
        return lax.psum(terms, axes)
    me = lax.axis_index("prow") * lax.axis_size("pcol") + lax.axis_index("pcol")
    value = terms.reshape(rows, terms.shape[2])
    bits = []
    bit = 1
    while bit < devices:
        bits.append(bit)
        bit *= 2
    for bit in bits:
        low = (me // bit) % 2 == 0
        half = value.shape[0] // 2
        keep = jnp.where(low, value[:half], value[half:])
        send = jnp.where(low, value[half:], value[:half])
        value = keep + lax.ppermute(send, axes, [(d, d ^ bit) for d in range(devices)])
    value = value.astype(jnp.bfloat16)
    for bit in reversed(bits):
        low = (me // bit) % 2 == 0
        got = lax.ppermute(value, axes, [(d, d ^ bit) for d in range(devices)])
        value = jnp.concatenate(
            [jnp.where(low, value, got), jnp.where(low, got, value)], axis=0
        )
    return value.astype(jnp.float32).reshape(terms.shape)


def general(inverse_tiles, panel_blocks, pivot_inverse, diagonal_inverse, ancestors):
    seg_rows = panel_blocks.shape[0]
    n_super = pivot_inverse.shape[0]
    width = pivot_inverse.shape[1]
    row_devices = lax.axis_size("prow")
    col_devices = lax.axis_size("pcol")
    segment = lax.axis_index("prow") * col_devices + lax.axis_index("pcol")
    row_ids = segment * seg_rows + lax.iota(jnp.int32, seg_rows)
    block_ids = row_ids // width
    listed = jnp.any(block_ids[:, None, None] == ancestors[None, :, :], axis=2).astype(jnp.float32)
    route = []
    for s in range(row_devices * col_devices):
        route.append((s, (s % row_devices) * col_devices + s // row_devices))
    crosses, terms, panels, scaled = [], [], [], []
    for k in range(n_super):
        normed = jnp.dot(
            panel_blocks[:, k * width:(k + 1) * width], pivot_inverse[k],
            preferred_element_type=jnp.float32,
        )
        own = (normed * listed[:, k:k + 1]).astype(jnp.bfloat16)
        scaled.append(own)
        moved = lax.ppermute(own, ("prow", "pcol"), route)
        panels.append(lax.all_gather(moved, "prow", axis=0, tiled=True))
    for k in range(n_super):
        product = jnp.dot(inverse_tiles, panels[k], preferred_element_type=jnp.float32)
        cross = -(reduce_rows(product, seg_rows) * listed[:, k:k + 1])
        crosses.append(cross)
        terms.append(lax.dot_general(
            scaled[k].astype(jnp.float32), cross, (((0,), (0,)), ((), ())),
            precision=lax.Precision.HIGHEST,
        ))
    diagonal = diagonal_inverse - sum_everywhere(jnp.stack(terms))
    return (jnp.concatenate(crosses, axis=1), diagonal)


def remote(src, dst, send, recv, device):
    return pltpu.make_async_remote_copy(
        src_ref=src, dst_ref=dst, send_sem=send, recv_sem=recv,
        device_id=device, device_id_type=MESH,
    )


def gather_kernel(nz, ny, nc, n_super, chunk, steps, place, own, out, dense, lane,
                  s1, r1, su, sd, rz, sp, ro, sy):
    lanes = ny * nc
    per = own.shape[1]
    halves = lane.shape[2]
    p, c = lax.axis_index("prow"), lax.axis_index("pcol")
    z, y = p // ny, lax.rem(p, ny)
    e = y * nc + c

    def peer(o):
        other = lax.rem(e + o, lanes)
        return other, (z * ny + other // nc, lax.rem(other, nc))

    barrier = pltpu.get_barrier_semaphore()
    for o in range(1, lanes):
        pl.semaphore_signal(barrier, inc=1, device_id=peer(o)[1], device_id_type=MESH)

    @pl.when(z > 0)
    def _():
        pl.semaphore_signal(barrier, inc=1, device_id=(p - ny, c), device_id_type=MESH)

    @pl.when(z < nz - 1)
    def _():
        pl.semaphore_signal(barrier, inc=1, device_id=(p + ny, c), device_id_type=MESH)

    near = jnp.where(z > 0, 1, 0) + jnp.where(z < nz - 1, 1, 0)
    pl.semaphore_wait(barrier, lanes - 1 + near)

    def deal(o):
        other, device = peer(o)
        return remote(own.at[other], dense.at[pl.ds(e * per, per)], s1.at[o], r1.at[e], device)

    for o in range(1, lanes):
        deal(o).start()
    home = pltpu.make_async_copy(own.at[e], dense.at[pl.ds(e * per, per)], r1.at[e])
    home.start()
    home.wait()
    for o in range(1, lanes):
        other, device = peer(o)
        part = dense.at[pl.ds(other * per, per)]
        remote(part, part, s1.at[o], r1.at[other], device).wait_recv()

    def span(t):
        return pl.ds(t * chunk, chunk)

    def up(g, t):
        part = lane.at[g, span(t)]
        return remote(part, part, su.at[g, t], rz.at[g, t], (p + ny, c))

    def down(g, t):
        part = lane.at[g, span(t)]
        return remote(part, part, sd.at[g, t], rz.at[g, t], (p - ny, c))

    def cross_plane(g, t):
        return remote(lane.at[g, span(t)], out.at[span(t), :, e], sp.at[g, t], ro.at[e, t], (p, g))

    def stay(t):
        return pltpu.make_async_copy(lane.at[c, span(t)], out.at[span(t), :, e], sp.at[c, t])

    def across(l, o, t):
        part = out.at[span(t), :, y * nc + l]
        return remote(part, part, sy.at[l, o - 1, t], ro.at[y * nc + l, t],
                      (z * ny + lax.rem(y + o, ny), c))

    def arrived(other, t):
        part = out.at[span(t), :, other]
        remote(part, part, sp.at[0, t], ro.at[other, t], (p, c)).wait_recv()

    def spread(g, t):
        @pl.when(jnp.logical_and(g <= z, z < nz - 1))
        def _():
            up(g, t).start()

        @pl.when(jnp.logical_and(g >= z, z > 0))
        def _():
            down(g, t).start()

        @pl.when(g != c)
        def _():
            cross_plane(g, t).start()

        @pl.when(g == c)
        def _():
            stay(t).start()

    away = jnp.maximum(z - c, c - z)

    def step(tau, carry):
        @pl.when(tau < steps)
        def _():
            def pack(i, carry):
                s = tau * chunk + i
                at = place[s]
                for h in range(halves):
                    lane[z, s, h] = dense[at + h * n_super]
                return carry
            lax.fori_loop(0, chunk, pack, 0)
            spread(z, tau)

        for d in range(1, nz):
            t = tau - d
            live = jnp.logical_and(t >= 0, t < steps)
            for g, ok in ((z - d, z - d >= 0), (z + d, z + d < nz)):
                @pl.when(jnp.logical_and(live, ok))
                def _():
                    part = lane.at[g, span(t)]
                    remote(part, part, su.at[g, t], rz.at[g, t], (p, c)).wait_recv()
                    spread(g, t)

        t = tau - 1 - away

        @pl.when(jnp.logical_and(t >= 0, t < steps))
        def _():
            for l in range(nc):
                @pl.when(l == c)
                def _():
                    stay(t).wait()

                @pl.when(l != c)
                def _():
                    arrived(y * nc + l, t)

                for o in range(1, ny):
                    across(l, o, t).start()
        return carry

    lax.fori_loop(0, steps + nz, step, 0)

    def finish(t, carry):
        for o in range(1, ny):
            for l in range(nc):
                arrived(lax.rem(y + o, ny) * nc + l, t)
        for o in range(1, ny):
            for l in range(nc):
                across(l, o, t).wait_send()
        for g in range(nz):
            @pl.when(jnp.logical_and(g <= z, z < nz - 1))
            def _():
                up(g, t).wait_send()

            @pl.when(jnp.logical_and(g >= z, z > 0))
            def _():
                down(g, t).wait_send()

            @pl.when(g != c)
            def _():
                cross_plane(g, t).wait_send()
        return carry

    lax.fori_loop(0, steps, finish, 0)
    for o in range(1, lanes):
        deal(o).wait_send()


def multiply_kernel(member, tiles, recv, out, buf, held, acc, js, at_k, at_r, at_j, at_s, ends,
                    asem, hsem):
    n_super, row_blocks, width = out.shape[:3]
    col_blocks = js.shape[0]
    slots, depth = held.shape[0], buf.shape[0]
    first_row = lax.axis_index("prow") * row_blocks
    first_col = lax.axis_index("pcol") * col_blocks

    def slot(s):
        return pltpu.make_async_copy(recv.at[s], held.at[s], hsem.at[s])

    def fetch(i):
        rows = pl.ds(pl.multiple_of(at_r[i] * width, width), width)
        cols = pl.ds(pl.multiple_of(at_j[i] * width, width), width)
        at = lax.rem(i, depth)
        return pltpu.make_async_copy(tiles.at[rows, cols], buf.at[at], asem.at[at])

    def begin(s, carry):
        slot(s).start()
        return carry

    lax.fori_loop(0, slots, begin, 0)

    def of_super(k, carry):
        n, base = carry

        def column(j, count):
            js[count] = j
            return count + member[(first_col + j) * n_super + k]

        count = lax.fori_loop(0, col_blocks, column, 0)

        def row(r, n):
            live = jnp.where(member[(first_row + r) * n_super + k] > 0, count, 0)

            def one(i, n):
                at_k[n], at_r[n], at_j[n], at_s[n] = k, r, js[i], base + i
                ends[n] = jnp.where(i == 0, 1, 0) + jnp.where(i == count - 1, 2, 0)
                return n + 1

            @pl.when(live == 0)
            def _():
                out[k, r] = jnp.zeros(out.shape[2:], out.dtype)

            return lax.fori_loop(0, live, one, n)

        return lax.fori_loop(0, row_blocks, row, n), base + count

    n, _ = lax.fori_loop(0, n_super, of_super, (0, 0))

    def early(i, carry):
        fetch(i).start()
        return carry

    lax.fori_loop(0, jnp.minimum(n, depth - 1), early, 0)

    def ready(s, carry):
        slot(s).wait()
        return carry

    def item(i, seen):
        @pl.when(i + depth - 1 < n)
        def _():
            fetch(i + depth - 1).start()

        s, end = at_s[i], ends[i]
        lax.fori_loop(seen, s + 1, ready, 0)
        fetch(i).wait()
        product = jnp.dot(buf[lax.rem(i, depth)], held[s], preferred_element_type=jnp.float32)

        @pl.when(end % 2 == 1)
        def _():
            acc[...] = product

        @pl.when(end % 2 == 0)
        def _():
            acc[...] += product

        @pl.when(end >= 2)
        def _():
            out[at_k[i], at_r[i]] = acc[...].astype(out.dtype)

        return jnp.maximum(seen, s + 1)

    seen = lax.fori_loop(0, n, item, 0)
    lax.fori_loop(seen, slots, ready, 0)


def finish_kernel(nr, nc, listed, scaled, diag, part, cross_out, diag_out, mine, cbuf, xs, xbuf,
                  cross, term, hbuf, sbuf, pbuf, gbuf, lm, sc, rc, sx, rx, so, sh, rh, sq, rq,
                  sg, rg, sf, rf):
    n_super, width = diag.shape[0], diag.shape[1]
    chips, piece = pbuf.shape[1], pbuf.shape[2]
    half = width // 2
    parts = 3
    rows = mine.shape[2] // parts
    p, c = lax.axis_index("prow"), lax.axis_index("pcol")
    x, core = c // 2, lax.rem(c, 2)
    me = p * (nc // 2) + x
    beside = (p, x * 2 + 1 - core)
    opposite = (p, (1 - x) * 2 + core)

    def chip(o):
        other = lax.rem(me + o, chips)
        return other, (other // (nc // 2), lax.rem(other, nc // 2) * 2 + core)

    barrier = pltpu.get_barrier_semaphore()
    pl.semaphore_signal(barrier, inc=1, device_id=beside, device_id_type=MESH)
    for o in range(1, chips):
        pl.semaphore_signal(barrier, inc=1, device_id=chip(o)[1], device_id_type=MESH)

    def load(k, w):
        seg = jnp.where(w == 0, 1 - x, x) * 2 + core
        return pltpu.make_async_copy(part.at[k, seg], mine.at[k, w], lm.at[k, w])

    for k in range(n_super):
        load(k, 0).start()
    for k in range(n_super):
        load(k, 1).start()
    pl.semaphore_wait(barrier, chips)

    def to_core(k, w):
        seg = jnp.where(w == 0, 1 - x, x) * 2 + 1 - core
        return remote(part.at[k, seg], cbuf.at[k, w], sc.at[k, w], rc.at[k, w], beside)

    def to_x(k):
        return remote(xs.at[k], xbuf.at[k], sx.at[k], rx.at[k], opposite)

    def store(k):
        return pltpu.make_async_copy(cross.at[k], cross_out.at[:, pl.ds(k * width, width)], so.at[k])

    def to_half(k):
        return remote(term.at[k, 1 - core], hbuf.at[k], sh.at[k], rh.at[k], beside)

    def to_piece(k, o):
        other, device = chip(o)
        return remote(sbuf.at[k, other], pbuf.at[k, me], sq.at[k, o], rq.at[k, me], device)

    def to_all(k, o):
        _, device = chip(o)
        ref = gbuf.at[k, core, me]
        return remote(ref, ref, sg.at[k, o], rg.at[k, me], device)

    def to_pair(k):
        ref = gbuf.at[k, core]
        return remote(ref, ref, sf.at[k], rf.at[k], beside)

    for k in range(n_super):
        to_core(k, 0).start()
    for k in range(n_super):
        load(k, 0).wait()
        to_core(k, 0).wait_recv()
        to_core(k, 1).start()

        def half_sum(i, carry):
            at = pl.ds(pl.multiple_of(i * rows, rows), rows)
            total = mine[k, 0, at].astype(jnp.float32) + cbuf[k, 0, at].astype(jnp.float32)
            xs[k, at] = total.astype(jnp.bfloat16)
            return carry

        lax.fori_loop(0, parts, half_sum, 0)
        to_x(k).start()

    def own_sum(k):
        load(k, 1).wait()
        to_core(k, 1).wait_recv()
        to_x(k).wait_recv()
        term[k] = jnp.zeros(term.shape[1:], jnp.float32)

        def add(i, carry):
            at = pl.ds(pl.multiple_of(i * rows, rows), rows)
            total = mine[k, 1, at].astype(jnp.float32) + cbuf[k, 1, at].astype(jnp.float32)
            total = -((total + xbuf[k, at].astype(jnp.float32)) * listed[at, k:k + 1])
            cross[k, at] = total
            high = total.astype(jnp.bfloat16)
            low = (total - high.astype(jnp.float32)).astype(jnp.bfloat16)
            left = scaled[at, k * width:(k + 1) * width]
            dims = (((0,), (0,)), ((), ()))
            both = lax.dot_general(left, high, dims, preferred_element_type=jnp.float32)
            both += lax.dot_general(left, low, dims, preferred_element_type=jnp.float32)
            term[k] += both.reshape(2, half, width)
            return carry

        lax.fori_loop(0, parts, add, 0)
        to_half(k).start()
        store(k).start()

    def deal(k):
        to_half(k).wait_recv()
        sbuf[k] = (term[k, core] + hbuf[k]).reshape(chips, piece, width)
        for o in range(1, chips):
            to_piece(k, o).start()

    def collect(k):
        total = sbuf[k, me]
        for o in range(1, chips):
            other, device = chip(o)
            remote(pbuf.at[k, other], pbuf.at[k, other], sq.at[k, o], rq.at[k, other], device).wait_recv()
            total = total + pbuf[k, other]
        gbuf[k, core, me] = total.astype(jnp.bfloat16)
        for o in range(1, chips):
            to_all(k, o).start()

    def pair(k):
        for o in range(1, chips):
            other, device = chip(o)
            ref = gbuf.at[k, core, other]
            remote(ref, ref, sg.at[k, o], rg.at[k, other], device).wait_recv()
        to_pair(k).start()

    def result(k):
        ref = gbuf.at[k, 1 - core]
        remote(ref, ref, sf.at[k], rf.at[k], beside).wait_recv()
        total = gbuf[k].astype(jnp.float32).reshape(width, width)
        diag_out[k] = diag[k] - total

    own_sum(0)
    deal(0)
    for k in range(1, n_super):
        own_sum(k)
        deal(k)
        collect(k - 1)
    collect(n_super - 1)
    for k in range(n_super):
        pair(k)
    for k in range(n_super):
        result(k)
    for k in range(n_super):
        for w in range(2):
            to_core(k, w).wait_send()
        to_x(k).wait_send()
        store(k).wait()
        to_half(k).wait_send()
        for o in range(1, chips):
            to_piece(k, o).wait_send()
            to_all(k, o).wait_send()
        to_pair(k).wait_send()


def squeeze(flags, size):
    flags = flags.astype(jnp.int32)
    where = jnp.arange(flags.shape[0])
    rank = jnp.sum(jnp.where(where[None, :] < where[:, None], flags[None, :], 0), axis=1)
    hit = jnp.logical_and(rank[None, :] == jnp.arange(size)[:, None], flags[None, :] > 0)
    index = jnp.sum(jnp.where(hit, where[None, :], 0), axis=1)
    return index.astype(jnp.int32)


def partial_products(slots, chunk, collective_id, ny, member, own, inverse_tiles):
    lanes, per, thin, width = own.shape
    n_super = member.shape[1]
    nr, nc = lax.axis_size("prow"), lax.axis_size("pcol")
    nz = nr // ny
    halves = width // (lanes * thin)
    row_blocks = inverse_tiles.shape[0] // width
    col_blocks = inverse_tiles.shape[1] // width

    z = lax.axis_index("prow") // ny
    of_plane = lax.dynamic_slice_in_dim(member, z * col_blocks, col_blocks, 0).T.reshape(-1)
    index = squeeze(of_plane, slots)
    place = index % col_blocks * (halves * n_super) + index // col_blocks
    steps = slots // chunk
    sems = [
        (lanes,), (lanes,), (nz, steps), (nz, steps), (nz, steps), (nz, steps), (lanes, steps),
        (nc, max(ny - 1, 1), steps),
    ]
    recv = pl.pallas_call(
        functools.partial(gather_kernel, nz, ny, nc, n_super, chunk, steps),
        out_shape=jax.ShapeDtypeStruct((slots, halves, lanes, thin, width), jnp.bfloat16),
        in_specs=[pl.BlockSpec(memory_space=pltpu.SMEM), pl.BlockSpec(memory_space=pl.ANY)],
        out_specs=pl.BlockSpec(memory_space=pl.ANY),
        scratch_shapes=[
            pltpu.VMEM((lanes * per, thin, width), jnp.bfloat16),
            pltpu.VMEM((nz, slots, halves, thin, width), jnp.bfloat16),
        ] + [pltpu.SemaphoreType.DMA(s) for s in sems],
        compiler_params=pltpu.CompilerParams(
            collective_id=collective_id, has_side_effects=True, vmem_limit_bytes=40 * 2**20,
        ),
        name="gather_listed",
    )(place, own)
    recv = recv.reshape(slots, width, width)

    most = n_super * row_blocks * col_blocks
    return pl.pallas_call(
        multiply_kernel,
        out_shape=jax.ShapeDtypeStruct((n_super, row_blocks, width, width), jnp.bfloat16),
        in_specs=[pl.BlockSpec(memory_space=pltpu.SMEM)] + [pl.BlockSpec(memory_space=pl.ANY)] * 2,
        out_specs=pl.BlockSpec(memory_space=pltpu.VMEM),
        scratch_shapes=[
            pltpu.VMEM((DEPTH, width, width), jnp.bfloat16),
            pltpu.VMEM((slots, width, width), jnp.bfloat16),
            pltpu.VMEM((width, width), jnp.float32),
            pltpu.SMEM((col_blocks,), jnp.int32),
        ] + [pltpu.SMEM((most,), jnp.int32)] * 5 + [
            pltpu.SemaphoreType.DMA((DEPTH,)),
            pltpu.SemaphoreType.DMA((slots,)),
        ],
        compiler_params=pltpu.CompilerParams(vmem_limit_bytes=48 * 2**20),
        name="multiply_listed",
    )(member.reshape(-1).astype(jnp.int32), inverse_tiles, recv)


def on_device(inverse_tiles, panel_blocks, pivot_inverse, diagonal_inverse, ancestors):
    nr, nc = lax.axis_size("prow"), lax.axis_size("pcol")
    n_super, width = pivot_inverse.shape[0], pivot_inverse.shape[1]
    seg_rows = panel_blocks.shape[0]
    ny = nr // nc
    lanes, chips = ny * nc, nr * 2
    sub = math.gcd(seg_rows, width)
    fits = (
        nr == lanes and nc == 4 and sub % (lanes * 16) == 0 and seg_rows % 3 == 0
        and width % (chips * 32) == 0
        and inverse_tiles.shape[0] % width == 0 and inverse_tiles.shape[1] % width == 0
    )
    if not fits:
        return general(inverse_tiles, panel_blocks, pivot_inverse, diagonal_inverse, ancestors)
    blocks = nr * nc * seg_rows // width
    member = jnp.any(jnp.arange(blocks)[:, None, None] == ancestors[None, :, :], axis=2)

    segment = lax.axis_index("prow") * nc + lax.axis_index("pcol")
    block_ids = (segment * seg_rows + lax.iota(jnp.int32, seg_rows)) // width
    listed = jnp.any(block_ids[:, None, None] == ancestors[None, :, :], axis=2).astype(jnp.float32)
    scaled = []
    for k in range(n_super):
        normed = jnp.dot(
            panel_blocks[:, k * width:(k + 1) * width], pivot_inverse[k],
            preferred_element_type=jnp.float32,
        )
        scaled.append((normed * listed[:, k:k + 1]).astype(jnp.bfloat16))
    scaled = jnp.concatenate(scaled, axis=1)
    parts, thin = seg_rows // sub, sub // lanes
    own = scaled.reshape(parts, lanes, thin, n_super, width).transpose(1, 0, 3, 2, 4)
    own = own.reshape(lanes, parts * n_super, thin, width)

    every = blocks // nc * n_super
    sizes = [(every * 11 // 18, 2), (every, 4)]
    sizes = [(s - s % chunk, chunk) for s, chunk in sizes]
    largest = jnp.max(jnp.sum(member.reshape(nc, -1).astype(jnp.int32), axis=1))
    level = sum((largest > s).astype(jnp.int32) for s, _ in sizes[:-1])
    branches = [
        functools.partial(partial_products, s, chunk, i + 1, ny)
        for i, (s, chunk) in enumerate(sizes)
    ]
    part = lax.switch(level, branches, member, own, inverse_tiles)
    part = part.reshape(n_super, nc, seg_rows, width)

    piece = width // 2 // chips
    bf16, f32 = jnp.bfloat16, jnp.float32
    k2 = (n_super, 2, seg_rows, width)
    k1 = (n_super, seg_rows, width)
    scratch = [
        (k2, bf16), (k2, bf16), (k1, bf16), (k1, bf16), (k1, f32),
        ((n_super, 2, width // 2, width), f32), ((n_super, width // 2, width), f32),
        ((n_super, chips, piece, width), f32), ((n_super, chips, piece, width), f32),
        ((n_super, 2, chips, piece, width), bf16),
    ]
    one, two, many = (n_super,), (n_super, 2), (n_super, chips)
    sems = [two, two, two, one, one, one, one, one, many, many, many, many, one, one]
    return pl.pallas_call(
        functools.partial(finish_kernel, nr, nc),
        out_shape=(
            jax.ShapeDtypeStruct((seg_rows, n_super * width), f32),
            jax.ShapeDtypeStruct((n_super, width, width), f32),
        ),
        in_specs=[pl.BlockSpec(memory_space=pltpu.VMEM)] * 3 + [pl.BlockSpec(memory_space=pl.ANY)],
        out_specs=(pl.BlockSpec(memory_space=pl.ANY), pl.BlockSpec(memory_space=pltpu.VMEM)),
        scratch_shapes=[pltpu.VMEM(s, t) for s, t in scratch]
        + [pltpu.SemaphoreType.DMA(s) for s in sems],
        compiler_params=pltpu.CompilerParams(
            collective_id=0, has_side_effects=True, vmem_limit_bytes=56 * 2**20,
        ),
        name="sum_and_finish",
    )(listed, scaled, diagonal_inverse, part)


def solution(mesh):
    in_specs = (P("prow", "pcol"), P(("prow", "pcol"), None), P(), P(), P())
    out_specs = (P(("prow", "pcol"), None), P())
    return jax.shard_map(
        on_device, mesh=mesh, in_specs=in_specs, out_specs=out_specs, check_vma=False
    )
```

```python
import functools
import math

import jax
import jax.numpy as jnp
from jax import lax
from jax.experimental import pallas as pl
from jax.experimental.pallas import tpu as pltpu
from jax.sharding import PartitionSpec as P

MESH = pl.DeviceIdType.MESH
DEPTH = 6


def reduce_rows(partial, seg_rows):
    devices = lax.axis_size("pcol")
    width = partial.shape[1]
    me = lax.axis_index("pcol")
    if devices & (devices - 1):
        return lax.psum_scatter(partial, "pcol", scatter_dimension=0, tiled=True)
    value = partial.reshape(devices, seg_rows, width)
    bit = 1
    while bit < devices:
        mine = (me // bit) % 2
        halves = value.reshape(value.shape[0] // 2, 2, seg_rows, width)
        keep = jnp.where(mine == 0, halves[:, 0], halves[:, 1])
        send = jnp.where(mine == 0, halves[:, 1], halves[:, 0]).astype(jnp.bfloat16)
        got = lax.ppermute(send, "pcol", [(d, d ^ bit) for d in range(devices)])
        value = keep + got.astype(jnp.float32)
        bit *= 2
    return value.reshape(seg_rows, width)


def sum_everywhere(terms):
    axes = ("prow", "pcol")
    devices = lax.axis_size("prow") * lax.axis_size("pcol")
    rows = terms.shape[0] * terms.shape[1]
    if devices & (devices - 1) or rows % devices:
        return lax.psum(terms, axes)
    me = lax.axis_index("prow") * lax.axis_size("pcol") + lax.axis_index("pcol")
    value = terms.reshape(rows, terms.shape[2])
    bits = []
    bit = 1
    while bit < devices:
        bits.append(bit)
        bit *= 2
    for bit in bits:
        low = (me // bit) % 2 == 0
        half = value.shape[0] // 2
        keep = jnp.where(low, value[:half], value[half:])
        send = jnp.where(low, value[half:], value[:half])
        value = keep + lax.ppermute(send, axes, [(d, d ^ bit) for d in range(devices)])
    value = value.astype(jnp.bfloat16)
    for bit in reversed(bits):
        low = (me // bit) % 2 == 0
        got = lax.ppermute(value, axes, [(d, d ^ bit) for d in range(devices)])
        value = jnp.concatenate(
            [jnp.where(low, value, got), jnp.where(low, got, value)], axis=0
        )
    return value.astype(jnp.float32).reshape(terms.shape)


def general(inverse_tiles, panel_blocks, pivot_inverse, diagonal_inverse, ancestors):
    seg_rows = panel_blocks.shape[0]
    n_super = pivot_inverse.shape[0]
    width = pivot_inverse.shape[1]
    row_devices = lax.axis_size("prow")
    col_devices = lax.axis_size("pcol")
    segment = lax.axis_index("prow") * col_devices + lax.axis_index("pcol")
    row_ids = segment * seg_rows + lax.iota(jnp.int32, seg_rows)
    block_ids = row_ids // width
    listed = jnp.any(block_ids[:, None, None] == ancestors[None, :, :], axis=2).astype(jnp.float32)
    route = []
    for s in range(row_devices * col_devices):
        route.append((s, (s % row_devices) * col_devices + s // row_devices))
    crosses, terms, panels, scaled = [], [], [], []
    for k in range(n_super):
        normed = jnp.dot(
            panel_blocks[:, k * width:(k + 1) * width], pivot_inverse[k],
            preferred_element_type=jnp.float32,
        )
        own = (normed * listed[:, k:k + 1]).astype(jnp.bfloat16)
        scaled.append(own)
        moved = lax.ppermute(own, ("prow", "pcol"), route)
        panels.append(lax.all_gather(moved, "prow", axis=0, tiled=True))
    for k in range(n_super):
        product = jnp.dot(inverse_tiles, panels[k], preferred_element_type=jnp.float32)
        cross = -(reduce_rows(product, seg_rows) * listed[:, k:k + 1])
        crosses.append(cross)
        terms.append(lax.dot_general(
            scaled[k].astype(jnp.float32), cross, (((0,), (0,)), ((), ())),
            precision=lax.Precision.HIGHEST,
        ))
    diagonal = diagonal_inverse - sum_everywhere(jnp.stack(terms))
    return (jnp.concatenate(crosses, axis=1), diagonal)


def remote(src, dst, send, recv, device):
    return pltpu.make_async_remote_copy(
        src_ref=src, dst_ref=dst, send_sem=send, recv_sem=recv,
        device_id=device, device_id_type=MESH,
    )


def gather_kernel(nz, ny, nc, n_super, chunk, steps, place, listed, panel, pivot, out, scaled,
                  own, dense, lane, s1, r1, su, sd, rz, sp, ro, sy):
    lanes = ny * nc
    per, thin, width = own.shape[1:]
    parts, sub = per // n_super, thin * lanes
    halves = lane.shape[2]
    p, c = lax.axis_index("prow"), lax.axis_index("pcol")
    z, y = p // ny, lax.rem(p, ny)
    e = y * nc + c

    def peer(o):
        other = lax.rem(e + o, lanes)
        return other, (z * ny + other // nc, lax.rem(other, nc))

    barrier = pltpu.get_barrier_semaphore()
    for o in range(1, lanes):
        pl.semaphore_signal(barrier, inc=1, device_id=peer(o)[1], device_id_type=MESH)

    @pl.when(z > 0)
    def _():
        pl.semaphore_signal(barrier, inc=1, device_id=(p - ny, c), device_id_type=MESH)

    @pl.when(z < nz - 1)
    def _():
        pl.semaphore_signal(barrier, inc=1, device_id=(p + ny, c), device_id_type=MESH)

    near = jnp.where(z > 0, 1, 0) + jnp.where(z < nz - 1, 1, 0)

    def deal(b, o):
        other, device = peer(o)
        return remote(own.at[other, pl.ds(b * n_super, n_super)],
                      dense.at[pl.ds(e * per + b * n_super, n_super)],
                      s1.at[b, o], r1.at[b, e], device)

    def home(b):
        return pltpu.make_async_copy(own.at[e, pl.ds(b * n_super, n_super)],
                                     dense.at[pl.ds(e * per + b * n_super, n_super)], r1.at[b, e])

    for b in range(parts):
        rows = slice(b * sub, (b + 1) * sub)
        for k in range(n_super):
            cols = slice(k * width, (k + 1) * width)
            normed = jnp.dot(panel[rows, cols], pivot[k], preferred_element_type=jnp.float32)
            normed = (normed * listed[rows, k:k + 1]).astype(jnp.bfloat16)
            scaled[rows, cols] = normed
            own[:, b * n_super + k] = normed.reshape(lanes, thin, width)
        if b == 0:
            pl.semaphore_wait(barrier, lanes - 1 + near)
        for o in range(1, lanes):
            deal(b, o).start()
        home(b).start()
    for b in range(parts):
        home(b).wait()
        for o in range(1, lanes):
            other, device = peer(o)
            part = dense.at[pl.ds(other * per + b * n_super, n_super)]
            remote(part, part, s1.at[b, o], r1.at[b, other], device).wait_recv()

    def span(t):
        return pl.ds(t * chunk, chunk)

    def up(g, t):
        part = lane.at[g, span(t)]
        return remote(part, part, su.at[g, t], rz.at[g, t], (p + ny, c))

    def down(g, t):
        part = lane.at[g, span(t)]
        return remote(part, part, sd.at[g, t], rz.at[g, t], (p - ny, c))

    def cross_plane(g, t):
        return remote(lane.at[g, span(t)], out.at[span(t), :, e], sp.at[g, t], ro.at[e, t], (p, g))

    def stay(t):
        return pltpu.make_async_copy(lane.at[c, span(t)], out.at[span(t), :, e], sp.at[c, t])

    def across(l, o, t):
        part = out.at[span(t), :, y * nc + l]
        return remote(part, part, sy.at[l, o - 1, t], ro.at[y * nc + l, t],
                      (z * ny + lax.rem(y + o, ny), c))

    def arrived(other, t):
        part = out.at[span(t), :, other]
        remote(part, part, sp.at[0, t], ro.at[other, t], (p, c)).wait_recv()

    def spread(g, t):
        @pl.when(jnp.logical_and(g <= z, z < nz - 1))
        def _():
            up(g, t).start()

        @pl.when(jnp.logical_and(g >= z, z > 0))
        def _():
            down(g, t).start()

        @pl.when(g != c)
        def _():
            cross_plane(g, t).start()

        @pl.when(g == c)
        def _():
            stay(t).start()

    away = jnp.maximum(z - c, c - z)

    def step(tau, carry):
        @pl.when(tau < steps)
        def _():
            def pack(i, carry):
                s = tau * chunk + i
                at = place[s]
                for h in range(halves):
                    lane[z, s, h] = dense[at + h * n_super]
                return carry
            lax.fori_loop(0, chunk, pack, 0)
            spread(z, tau)

        for d in range(1, nz):
            t = tau - d
            live = jnp.logical_and(t >= 0, t < steps)
            for g, ok in ((z - d, z - d >= 0), (z + d, z + d < nz)):
                @pl.when(jnp.logical_and(live, ok))
                def _():
                    part = lane.at[g, span(t)]
                    remote(part, part, su.at[g, t], rz.at[g, t], (p, c)).wait_recv()
                    spread(g, t)

        t = tau - 1 - away

        @pl.when(jnp.logical_and(t >= 0, t < steps))
        def _():
            for l in range(nc):
                @pl.when(l == c)
                def _():
                    stay(t).wait()

                @pl.when(l != c)
                def _():
                    arrived(y * nc + l, t)

                for o in range(1, ny):
                    across(l, o, t).start()
        return carry

    lax.fori_loop(0, steps + nz, step, 0)

    def finish(t, carry):
        for o in range(1, ny):
            for l in range(nc):
                arrived(lax.rem(y + o, ny) * nc + l, t)
        for o in range(1, ny):
            for l in range(nc):
                across(l, o, t).wait_send()
        for g in range(nz):
            @pl.when(jnp.logical_and(g <= z, z < nz - 1))
            def _():
                up(g, t).wait_send()

            @pl.when(jnp.logical_and(g >= z, z > 0))
            def _():
                down(g, t).wait_send()

            @pl.when(g != c)
            def _():
                cross_plane(g, t).wait_send()
        return carry

    lax.fori_loop(0, steps, finish, 0)
    for b in range(parts):
        for o in range(1, lanes):
            deal(b, o).wait_send()


def multiply_kernel(member, tiles, recv, out, buf, held, acc, js, at_k, at_r, at_j, at_s, ends,
                    asem, hsem):
    n_super, row_blocks, width = out.shape[:3]
    col_blocks = js.shape[0]
    slots, depth = held.shape[0], buf.shape[0]
    first_row = lax.axis_index("prow") * row_blocks
    first_col = lax.axis_index("pcol") * col_blocks

    def slot(s):
        return pltpu.make_async_copy(recv.at[s], held.at[s], hsem.at[s])

    def fetch(i):
        rows = pl.ds(pl.multiple_of(at_r[i] * width, width), width)
        cols = pl.ds(pl.multiple_of(at_j[i] * width, width), width)
        at = lax.rem(i, depth)
        return pltpu.make_async_copy(tiles.at[rows, cols], buf.at[at], asem.at[at])

    def begin(s, carry):
        slot(s).start()
        return carry

    lax.fori_loop(0, slots, begin, 0)

    def of_super(k, carry):
        n, base = carry

        def column(j, count):
            js[count] = j
            return count + member[(first_col + j) * n_super + k]

        count = lax.fori_loop(0, col_blocks, column, 0)

        def row(r, n):
            live = jnp.where(member[(first_row + r) * n_super + k] > 0, count, 0)

            def one(i, n):
                at_k[n], at_r[n], at_j[n], at_s[n] = k, r, js[i], base + i
                ends[n] = jnp.where(i == 0, 1, 0) + jnp.where(i == count - 1, 2, 0)
                return n + 1

            @pl.when(live == 0)
            def _():
                out[k, r] = jnp.zeros(out.shape[2:], out.dtype)

            return lax.fori_loop(0, live, one, n)

        return lax.fori_loop(0, row_blocks, row, n), base + count

    n, _ = lax.fori_loop(0, n_super, of_super, (0, 0))

    def early(i, carry):
        fetch(i).start()
        return carry

    lax.fori_loop(0, jnp.minimum(n, depth - 1), early, 0)

    def ready(s, carry):
        slot(s).wait()
        return carry

    def item(i, seen):
        @pl.when(i + depth - 1 < n)
        def _():
            fetch(i + depth - 1).start()

        s, end = at_s[i], ends[i]
        lax.fori_loop(seen, s + 1, ready, 0)
        fetch(i).wait()
        product = jnp.dot(buf[lax.rem(i, depth)], held[s], preferred_element_type=jnp.float32)

        @pl.when(end % 2 == 1)
        def _():
            acc[...] = product

        @pl.when(end % 2 == 0)
        def _():
            acc[...] += product

        @pl.when(end >= 2)
        def _():
            out[at_k[i], at_r[i]] = acc[...].astype(out.dtype)

        return jnp.maximum(seen, s + 1)

    seen = lax.fori_loop(0, n, item, 0)
    lax.fori_loop(seen, slots, ready, 0)


def finish_kernel(nr, nc, listed, scaled, diag, part, cross_out, diag_out, mine, cbuf, xs, xbuf,
                  cross, term, hbuf, sbuf, pbuf, gbuf, lm, sc, rc, sx, rx, so, sh, rh, sq, rq,
                  sg, rg, sf, rf):
    n_super, width = diag.shape[0], diag.shape[1]
    chips, piece = pbuf.shape[1], pbuf.shape[2]
    half = width // 2
    parts = 3
    rows = mine.shape[2] // parts
    p, c = lax.axis_index("prow"), lax.axis_index("pcol")
    x, core = c // 2, lax.rem(c, 2)
    me = p * (nc // 2) + x
    beside = (p, x * 2 + 1 - core)
    opposite = (p, (1 - x) * 2 + core)

    def chip(o):
        other = lax.rem(me + o, chips)
        return other, (other // (nc // 2), lax.rem(other, nc // 2) * 2 + core)

    barrier = pltpu.get_barrier_semaphore()
    pl.semaphore_signal(barrier, inc=1, device_id=beside, device_id_type=MESH)
    for o in range(1, chips):
        pl.semaphore_signal(barrier, inc=1, device_id=chip(o)[1], device_id_type=MESH)

    def load(k, w):
        seg = jnp.where(w == 0, 1 - x, x) * 2 + core
        return pltpu.make_async_copy(part.at[k, seg], mine.at[k, w], lm.at[k, w])

    for k in range(n_super):
        load(k, 0).start()
    for k in range(n_super):
        load(k, 1).start()
    pl.semaphore_wait(barrier, chips)

    def to_core(k, w):
        seg = jnp.where(w == 0, 1 - x, x) * 2 + 1 - core
        return remote(part.at[k, seg], cbuf.at[k, w], sc.at[k, w], rc.at[k, w], beside)

    def to_x(k):
        return remote(xs.at[k], xbuf.at[k], sx.at[k], rx.at[k], opposite)

    def store(k):
        return pltpu.make_async_copy(cross.at[k], cross_out.at[:, pl.ds(k * width, width)], so.at[k])

    def to_half(k):
        return remote(term.at[k, 1 - core], hbuf.at[k], sh.at[k], rh.at[k], beside)

    def to_piece(k, o):
        other, device = chip(o)
        return remote(sbuf.at[k, other], pbuf.at[k, me], sq.at[k, o], rq.at[k, me], device)

    def to_all(k, o):
        _, device = chip(o)
        ref = gbuf.at[k, core, me]
        return remote(ref, ref, sg.at[k, o], rg.at[k, me], device)

    def to_pair(k):
        ref = gbuf.at[k, core]
        return remote(ref, ref, sf.at[k], rf.at[k], beside)

    for k in range(n_super):
        to_core(k, 0).start()
    for k in range(n_super):
        load(k, 0).wait()
        to_core(k, 0).wait_recv()
        to_core(k, 1).start()

        def half_sum(i, carry):
            at = pl.ds(pl.multiple_of(i * rows, rows), rows)
            total = mine[k, 0, at].astype(jnp.float32) + cbuf[k, 0, at].astype(jnp.float32)
            xs[k, at] = total.astype(jnp.bfloat16)
            return carry

        lax.fori_loop(0, parts, half_sum, 0)
        to_x(k).start()

    def own_sum(k):
        load(k, 1).wait()
        to_core(k, 1).wait_recv()
        to_x(k).wait_recv()
        term[k] = jnp.zeros(term.shape[1:], jnp.float32)

        def add(i, carry):
            at = pl.ds(pl.multiple_of(i * rows, rows), rows)
            total = mine[k, 1, at].astype(jnp.float32) + cbuf[k, 1, at].astype(jnp.float32)
            total = -((total + xbuf[k, at].astype(jnp.float32)) * listed[at, k:k + 1])
            cross[k, at] = total
            high = total.astype(jnp.bfloat16)
            low = (total - high.astype(jnp.float32)).astype(jnp.bfloat16)
            left = scaled[at, k * width:(k + 1) * width]
            dims = (((0,), (0,)), ((), ()))
            both = lax.dot_general(left, high, dims, preferred_element_type=jnp.float32)
            both += lax.dot_general(left, low, dims, preferred_element_type=jnp.float32)
            term[k] += both.reshape(2, half, width)
            return carry

        lax.fori_loop(0, parts, add, 0)
        to_half(k).start()
        store(k).start()

    def deal(k):
        to_half(k).wait_recv()
        sbuf[k] = (term[k, core] + hbuf[k]).reshape(chips, piece, width)
        for o in range(1, chips):
            to_piece(k, o).start()

    def collect(k):
        total = sbuf[k, me]
        for o in range(1, chips):
            other, device = chip(o)
            remote(pbuf.at[k, other], pbuf.at[k, other], sq.at[k, o], rq.at[k, other], device).wait_recv()
            total = total + pbuf[k, other]
        gbuf[k, core, me] = total.astype(jnp.bfloat16)
        for o in range(1, chips):
            to_all(k, o).start()

    def pair(k):
        for o in range(1, chips):
            other, device = chip(o)
            ref = gbuf.at[k, core, other]
            remote(ref, ref, sg.at[k, o], rg.at[k, other], device).wait_recv()
        to_pair(k).start()

    def result(k):
        ref = gbuf.at[k, 1 - core]
        remote(ref, ref, sf.at[k], rf.at[k], beside).wait_recv()
        total = gbuf[k].astype(jnp.float32).reshape(width, width)
        diag_out[k] = diag[k] - total

    own_sum(0)
    deal(0)
    for k in range(1, n_super):
        own_sum(k)
        deal(k)
        collect(k - 1)
    collect(n_super - 1)
    for k in range(n_super):
        pair(k)
    for k in range(n_super):
        result(k)
    for k in range(n_super):
        for w in range(2):
            to_core(k, w).wait_send()
        to_x(k).wait_send()
        store(k).wait()
        to_half(k).wait_send()
        for o in range(1, chips):
            to_piece(k, o).wait_send()
            to_all(k, o).wait_send()
        to_pair(k).wait_send()


def squeeze(flags, size):
    flags = flags.astype(jnp.int32)
    where = jnp.arange(flags.shape[0])
    rank = jnp.sum(jnp.where(where[None, :] < where[:, None], flags[None, :], 0), axis=1)
    hit = jnp.logical_and(rank[None, :] == jnp.arange(size)[:, None], flags[None, :] > 0)
    index = jnp.sum(jnp.where(hit, where[None, :], 0), axis=1)
    return index.astype(jnp.int32)


def partial_products(slots, chunk, collective_id, ny, member, listed, panel_blocks, pivot_inverse,
                     inverse_tiles):
    n_super, width = pivot_inverse.shape[0], pivot_inverse.shape[1]
    seg_rows = panel_blocks.shape[0]
    nr, nc = lax.axis_size("prow"), lax.axis_size("pcol")
    nz, lanes = nr // ny, ny * nc
    sub = math.gcd(seg_rows, width)
    per, thin, halves = seg_rows // sub * n_super, sub // lanes, width // sub
    row_blocks = inverse_tiles.shape[0] // width
    col_blocks = inverse_tiles.shape[1] // width

    z = lax.axis_index("prow") // ny
    of_plane = lax.dynamic_slice_in_dim(member, z * col_blocks, col_blocks, 0).T.reshape(-1)
    index = squeeze(of_plane, slots)
    place = index % col_blocks * (halves * n_super) + index // col_blocks
    steps = slots // chunk
    sems = [
        (per // n_super, lanes), (per // n_super, lanes),
        (nz, steps), (nz, steps), (nz, steps), (nz, steps), (lanes, steps),
        (nc, max(ny - 1, 1), steps),
    ]
    vmem, hbm = pl.BlockSpec(memory_space=pltpu.VMEM), pl.BlockSpec(memory_space=pltpu.HBM)
    recv, scaled = pl.pallas_call(
        functools.partial(gather_kernel, nz, ny, nc, n_super, chunk, steps),
        out_shape=(
            jax.ShapeDtypeStruct((slots, halves, lanes, thin, width), jnp.bfloat16),
            jax.ShapeDtypeStruct(panel_blocks.shape, jnp.bfloat16),
        ),
        in_specs=[pl.BlockSpec(memory_space=pltpu.SMEM), vmem, vmem, vmem],
        out_specs=(hbm, vmem),
        scratch_shapes=[
            pltpu.VMEM((lanes, per, thin, width), jnp.bfloat16),
            pltpu.VMEM((lanes * per, thin, width), jnp.bfloat16),
            pltpu.VMEM((nz, slots, halves, thin, width), jnp.bfloat16),
        ] + [pltpu.SemaphoreType.DMA(s) for s in sems],
        compiler_params=pltpu.CompilerParams(
            collective_id=collective_id, has_side_effects=True, vmem_limit_bytes=40 * 2**20,
        ),
        name="gather_listed",
    )(place, listed, panel_blocks, pivot_inverse)
    recv = recv.reshape(slots, width, width)

    most = n_super * row_blocks * col_blocks
    part = pl.pallas_call(
        multiply_kernel,
        out_shape=jax.ShapeDtypeStruct((n_super, row_blocks, width, width), jnp.bfloat16),
        in_specs=[pl.BlockSpec(memory_space=pltpu.SMEM), hbm, hbm],
        out_specs=pl.BlockSpec(memory_space=pltpu.VMEM),
        scratch_shapes=[
            pltpu.VMEM((DEPTH, width, width), jnp.bfloat16),
            pltpu.VMEM((slots, width, width), jnp.bfloat16),
            pltpu.VMEM((width, width), jnp.float32),
            pltpu.SMEM((col_blocks,), jnp.int32),
        ] + [pltpu.SMEM((most,), jnp.int32)] * 5 + [
            pltpu.SemaphoreType.DMA((DEPTH,)),
            pltpu.SemaphoreType.DMA((slots,)),
        ],
        compiler_params=pltpu.CompilerParams(vmem_limit_bytes=48 * 2**20),
        name="multiply_listed",
    )(member.reshape(-1).astype(jnp.int32), inverse_tiles, recv)
    return part, scaled


def on_device(inverse_tiles, panel_blocks, pivot_inverse, diagonal_inverse, ancestors):
    nr, nc = lax.axis_size("prow"), lax.axis_size("pcol")
    n_super, width = pivot_inverse.shape[0], pivot_inverse.shape[1]
    seg_rows = panel_blocks.shape[0]
    ny = nr // nc
    lanes, chips = ny * nc, nr * 2
    sub = math.gcd(seg_rows, width)
    fits = (
        nr == lanes and nc == 4 and sub % (lanes * 16) == 0
        and (nr * nc * seg_rows // width * n_super) % (18 * nc) == 0 and seg_rows % 3 == 0
        and width % (chips * 32) == 0
        and inverse_tiles.shape[0] % width == 0 and inverse_tiles.shape[1] % width == 0
    )
    if not fits:
        return general(inverse_tiles, panel_blocks, pivot_inverse, diagonal_inverse, ancestors)
    blocks = nr * nc * seg_rows // width
    member = jnp.any(jnp.arange(blocks)[:, None, None] == ancestors[None, :, :], axis=2)

    segment = lax.axis_index("prow") * nc + lax.axis_index("pcol")
    block_ids = (segment * seg_rows + lax.iota(jnp.int32, seg_rows)) // width
    listed = jnp.any(block_ids[:, None, None] == ancestors[None, :, :], axis=2).astype(jnp.float32)
    every = blocks // nc * n_super
    sizes = [(every * n // 18, 1) for n in (10, 11, 12)] + [(every, 2)]
    largest = jnp.max(jnp.sum(member.reshape(nc, -1).astype(jnp.int32), axis=1))
    level = sum((largest > s).astype(jnp.int32) for s, _ in sizes[:-1])
    branches = [
        functools.partial(partial_products, s, chunk, i + 1, ny)
        for i, (s, chunk) in enumerate(sizes)
    ]
    part, scaled = lax.switch(
        level, branches, member, listed, panel_blocks, pivot_inverse, inverse_tiles)
    part = part.reshape(n_super, nc, seg_rows, width)

    piece = width // 2 // chips
    bf16, f32 = jnp.bfloat16, jnp.float32
    k2 = (n_super, 2, seg_rows, width)
    k1 = (n_super, seg_rows, width)
    scratch = [
        (k2, bf16), (k2, bf16), (k1, bf16), (k1, bf16), (k1, f32),
        ((n_super, 2, width // 2, width), f32), ((n_super, width // 2, width), f32),
        ((n_super, chips, piece, width), f32), ((n_super, chips, piece, width), f32),
        ((n_super, 2, chips, piece, width), bf16),
    ]
    one, two, many = (n_super,), (n_super, 2), (n_super, chips)
    sems = [two, two, two, one, one, one, one, one, many, many, many, many, one, one]
    return pl.pallas_call(
        functools.partial(finish_kernel, nr, nc),
        out_shape=(
            jax.ShapeDtypeStruct((seg_rows, n_super * width), f32),
            jax.ShapeDtypeStruct((n_super, width, width), f32),
        ),
        in_specs=[pl.BlockSpec(memory_space=pltpu.VMEM)] * 3 + [pl.BlockSpec(memory_space=pltpu.HBM)],
        out_specs=(pl.BlockSpec(memory_space=pl.ANY), pl.BlockSpec(memory_space=pltpu.VMEM)),
        scratch_shapes=[pltpu.VMEM(s, t) for s, t in scratch]
        + [pltpu.SemaphoreType.DMA(s) for s in sems],
        compiler_params=pltpu.CompilerParams(
            collective_id=0, has_side_effects=True, vmem_limit_bytes=56 * 2**20,
        ),
        name="sum_and_finish",
    )(listed, scaled, diagonal_inverse, part)


def solution(mesh):
    in_specs = (P("prow", "pcol"), P(("prow", "pcol"), None), P(), P(), P())
    out_specs = (P(("prow", "pcol"), None), P())
    return jax.shard_map(
        on_device, mesh=mesh, in_specs=in_specs, out_specs=out_specs, check_vma=False
    )
```

```python
import functools
import math

import jax
import jax.numpy as jnp
from jax import lax
from jax.experimental import pallas as pl
from jax.experimental.pallas import tpu as pltpu
from jax.sharding import PartitionSpec as P

MESH = pl.DeviceIdType.MESH


def reduce_rows(partial, seg_rows):
    devices = lax.axis_size("pcol")
    width = partial.shape[1]
    me = lax.axis_index("pcol")
    if devices & (devices - 1):
        return lax.psum_scatter(partial, "pcol", scatter_dimension=0, tiled=True)
    value = partial.reshape(devices, seg_rows, width)
    bit = 1
    while bit < devices:
        mine = (me // bit) % 2
        halves = value.reshape(value.shape[0] // 2, 2, seg_rows, width)
        keep = jnp.where(mine == 0, halves[:, 0], halves[:, 1])
        send = jnp.where(mine == 0, halves[:, 1], halves[:, 0]).astype(jnp.bfloat16)
        got = lax.ppermute(send, "pcol", [(d, d ^ bit) for d in range(devices)])
        value = keep + got.astype(jnp.float32)
        bit *= 2
    return value.reshape(seg_rows, width)


def sum_everywhere(terms):
    axes = ("prow", "pcol")
    devices = lax.axis_size("prow") * lax.axis_size("pcol")
    rows = terms.shape[0] * terms.shape[1]
    if devices & (devices - 1) or rows % devices:
        return lax.psum(terms, axes)
    me = lax.axis_index("prow") * lax.axis_size("pcol") + lax.axis_index("pcol")
    value = terms.reshape(rows, terms.shape[2])
    bits = []
    bit = 1
    while bit < devices:
        bits.append(bit)
        bit *= 2
    for bit in bits:
        low = (me // bit) % 2 == 0
        half = value.shape[0] // 2
        keep = jnp.where(low, value[:half], value[half:])
        send = jnp.where(low, value[half:], value[:half])
        value = keep + lax.ppermute(send, axes, [(d, d ^ bit) for d in range(devices)])
    value = value.astype(jnp.bfloat16)
    for bit in reversed(bits):
        low = (me // bit) % 2 == 0
        got = lax.ppermute(value, axes, [(d, d ^ bit) for d in range(devices)])
        value = jnp.concatenate(
            [jnp.where(low, value, got), jnp.where(low, got, value)], axis=0
        )
    return value.astype(jnp.float32).reshape(terms.shape)


def general(inverse_tiles, panel_blocks, pivot_inverse, diagonal_inverse, ancestors):
    seg_rows = panel_blocks.shape[0]
    n_super = pivot_inverse.shape[0]
    width = pivot_inverse.shape[1]
    row_devices = lax.axis_size("prow")
    col_devices = lax.axis_size("pcol")
    segment = lax.axis_index("prow") * col_devices + lax.axis_index("pcol")
    row_ids = segment * seg_rows + lax.iota(jnp.int32, seg_rows)
    block_ids = row_ids // width
    listed = jnp.any(block_ids[:, None, None] == ancestors[None, :, :], axis=2).astype(jnp.float32)
    route = []
    for s in range(row_devices * col_devices):
        route.append((s, (s % row_devices) * col_devices + s // row_devices))
    crosses, terms, panels, scaled = [], [], [], []
    for k in range(n_super):
        normed = jnp.dot(
            panel_blocks[:, k * width:(k + 1) * width], pivot_inverse[k],
            preferred_element_type=jnp.float32,
        )
        own = (normed * listed[:, k:k + 1]).astype(jnp.bfloat16)
        scaled.append(own)
        moved = lax.ppermute(own, ("prow", "pcol"), route)
        panels.append(lax.all_gather(moved, "prow", axis=0, tiled=True))
    for k in range(n_super):
        product = jnp.dot(inverse_tiles, panels[k], preferred_element_type=jnp.float32)
        cross = -(reduce_rows(product, seg_rows) * listed[:, k:k + 1])
        crosses.append(cross)
        terms.append(lax.dot_general(
            scaled[k].astype(jnp.float32), cross, (((0,), (0,)), ((), ())),
            precision=lax.Precision.HIGHEST,
        ))
    diagonal = diagonal_inverse - sum_everywhere(jnp.stack(terms))
    return (jnp.concatenate(crosses, axis=1), diagonal)


def remote(src, dst, send, recv, device):
    return pltpu.make_async_remote_copy(
        src_ref=src, dst_ref=dst, send_sem=send, recv_sem=recv,
        device_id=device, device_id_type=MESH,
    )


def deal_kernel(nz, ny, nc, n_super, place, listed, panel, pivot, packed, turned,
                own, dense, scaled, s1, r1):
    lanes = ny * nc
    per, thin, width = own.shape[1:]
    parts, sub = per // n_super, thin * lanes
    slots, halves = packed.shape[:2]
    p, c = lax.axis_index("prow"), lax.axis_index("pcol")
    z, y = p // ny, lax.rem(p, ny)
    e = y * nc + c

    def peer(o):
        other = lax.rem(e + o, lanes)
        return other, (z * ny + other // nc, lax.rem(other, nc))

    barrier = pltpu.get_barrier_semaphore()
    for o in range(1, lanes):
        pl.semaphore_signal(barrier, inc=1, device_id=peer(o)[1], device_id_type=MESH)

    def deal(b, o):
        other, device = peer(o)
        return remote(own.at[other, pl.ds(b * n_super, n_super)],
                      dense.at[pl.ds(e * per + b * n_super, n_super)],
                      s1.at[b, o], r1.at[b, e], device)

    def home(b):
        return pltpu.make_async_copy(own.at[e, pl.ds(b * n_super, n_super)],
                                     dense.at[pl.ds(e * per + b * n_super, n_super)], r1.at[b, e])

    for b in range(parts):
        rows = slice(b * sub, (b + 1) * sub)
        for k in range(n_super):
            cols = slice(k * width, (k + 1) * width)
            normed = jnp.dot(panel[rows, cols], pivot[k], preferred_element_type=jnp.float32)
            normed = (normed * listed[rows, k:k + 1]).astype(jnp.bfloat16)
            scaled[rows, cols] = normed
            own[:, b * n_super + k] = normed.reshape(lanes, thin, width)
        if b == 0:
            pl.semaphore_wait(barrier, lanes - 1)
        for o in range(1, lanes):
            deal(b, o).start()
        home(b).start()
    for b in range(parts):
        rows = slice(b * sub, (b + 1) * sub)
        for k in range(n_super):
            cols = slice(k * width, (k + 1) * width)
            turned[cols, rows] = scaled[rows, cols].astype(jnp.float32).T.astype(jnp.bfloat16)
    for b in range(parts):
        home(b).wait()
        for o in range(1, lanes):
            other, device = peer(o)
            part = dense.at[pl.ds(other * per + b * n_super, n_super)]
            remote(part, part, s1.at[b, o], r1.at[b, other], device).wait_recv()

    blank = dense.shape[0] - lanes * per
    dense[lanes * per:] = jnp.zeros((blank, thin, width), dense.dtype)

    def pack(s, carry):
        at = place[s]
        for h in range(halves):
            packed[s, h] = dense[at + h * n_super]
        return carry

    lax.fori_loop(0, slots, pack, 0)
    for b in range(parts):
        for o in range(1, lanes):
            deal(b, o).wait_send()


def main_kernel(nr, ny, nc, n_super, cap, depth, column, listed, turned, packed, diag, tiles,
                cross_out, diag_out, lane, *scratch):
    panels, scratch = scratch[:depth], scratch[depth:]
    main_body(nr, ny, nc, n_super, cap, column, listed, turned, packed, diag, tiles,
              cross_out, diag_out, lane, panels, *scratch)


def main_body(nr, ny, nc, n_super, cap, column, listed, turned, packed, diag, tiles,
              cross_out, diag_out, lane, panels,
              held, mine, cbuf, xbuf, cross, term, hbuf, sbuf, pbuf, gbuf,
              su, sd, rz, sp, ro, sy,
              sa, ld, sc, rc, sx, rx, so, sh, rh, sq, rq, sg, rg, sf, rf):
    nz, lanes = nr // ny, ny * nc
    steps = packed.shape[0]
    width = diag_out.shape[1]
    depth = len(panels)
    chips, piece = pbuf.shape[1], pbuf.shape[2]
    half = width // 2
    parts = 3
    seg_rows = cross.shape[1]
    rows = seg_rows // parts
    per_side = mine.shape[2] // width
    p, c = lax.axis_index("prow"), lax.axis_index("pcol")
    z, y = p // ny, lax.rem(p, ny)
    e = y * nc + c
    x, core = c // 2, lax.rem(c, 2)
    me = p * (nc // 2) + x
    beside = (p, x * 2 + 1 - core)
    opposite = (p, (1 - x) * 2 + core)

    def chip(o):
        other = lax.rem(me + o, chips)
        return other, (other // (nc // 2), lax.rem(other, nc // 2) * 2 + core)

    barrier = pltpu.get_barrier_semaphore()
    for o in range(1, chips):
        pl.semaphore_signal(barrier, inc=1, device_id=chip(o)[1], device_id_type=MESH)
    for i in range(nc // 2):
        pl.semaphore_signal(barrier, inc=1, device_id=(p, 2 * i + 1 - core), device_id_type=MESH)

    n_tiles = 2 * n_super * per_side

    class fetch:
        def __init__(self, t):
            side = 1 - x if t % (2 * per_side) < per_side else x
            at = pl.multiple_of((side * per_side + t % per_side) * width, width)
            self.copies = [
                pltpu.make_async_copy(
                    tiles.at[pl.ds(at, width), j * width:(j + 1) * width],
                    panels[t % depth].at[j], sa.at[t % depth, j])
                for j in range(panels[0].shape[0])
            ]

        def start(self):
            for copy in self.copies:
                copy.start()

        def wait(self):
            for copy in self.copies:
                copy.wait()

    given = pltpu.make_async_copy(diag, diag_out, ld.at[0])
    for t in range(max(depth - 1, 1)):
        fetch(t).start()
    given.start()
    pl.semaphore_wait(barrier, chips - 1 + nc // 2)

    def one(t):
        return pl.ds(t, 1)

    def spread(g, t, source):
        @pl.when(jnp.logical_and(g <= z, z < nz - 1))
        def _():
            remote(source, lane.at[g, one(t)], su.at[g, t], rz.at[g, t], (p + ny, c)).start()

        @pl.when(jnp.logical_and(g >= z, z > 0))
        def _():
            remote(source, lane.at[g, one(t)], sd.at[g, t], rz.at[g, t], (p - ny, c)).start()

        @pl.when(g != c)
        def _():
            remote(source, held.at[one(t), :, e], sp.at[g, t], ro.at[e, t], (p, g)).start()

        @pl.when(g == c)
        def _():
            pltpu.make_async_copy(source, held.at[one(t), :, e], sp.at[g, t]).start()

    def across(l, o, t):
        part = held.at[one(t), :, y * nc + l]
        return remote(part, part, sy.at[l, o - 1, t], ro.at[y * nc + l, t],
                      (z * ny + lax.rem(y + o, ny), c))

    def arrived(other, t):
        part = held.at[one(t), :, other]
        remote(part, part, sp.at[0, t], ro.at[other, t], beside).wait_recv()

    away = jnp.maximum(z - c, c - z)

    def step(tau, carry):
        @pl.when(tau < steps)
        def _():
            spread(z, tau, packed.at[one(tau)])

        for d in range(1, nz):
            t = tau - d
            live = jnp.logical_and(t >= 0, t < steps)
            for g, ok in ((z - d, z - d >= 0), (z + d, z + d < nz)):
                @pl.when(jnp.logical_and(live, ok))
                def _():
                    part = lane.at[g, one(t)]
                    remote(part, part, su.at[g, t], rz.at[g, t], beside).wait_recv()
                    spread(g, t, part)

        t = tau - 1 - away

        @pl.when(jnp.logical_and(t >= 0, t < steps))
        def _():
            for l in range(nc):
                @pl.when(l == c)
                def _():
                    part = held.at[one(t), :, e]
                    pltpu.make_async_copy(part, part, sp.at[c, t]).wait()

                @pl.when(l != c)
                def _():
                    arrived(y * nc + l, t)

                for o in range(1, ny):
                    across(l, o, t).start()
        return carry

    def complete(first, last):
        def wait(t, carry):
            for o in range(1, ny):
                for l in range(nc):
                    arrived(lax.rem(y + o, ny) * nc + l, t)
            return carry

        lax.fori_loop(first, last, wait, 0)

    def products(k, w, begin, end):
        for r in range(begin, end):
            t = (k * 2 + w) * per_side + r
            if depth > 1 and t + depth - 1 < n_tiles:
                fetch(t + depth - 1).start()
            fetch(t).wait()
            total = None
            for i in range(cap):
                block = held[k * cap + i].reshape(width, width)
                now = jnp.dot(panels[t % depth][column[k * cap + i]], block,
                              preferred_element_type=jnp.float32)
                total = now if total is None else total + now
            mine[k, w, r * width:(r + 1) * width] = total.astype(mine.dtype)
            if depth == 1 and t + 1 < n_tiles:
                fetch(t + 1).start()

    def seg(which):
        return pl.ds(pl.multiple_of(which * seg_rows, seg_rows), seg_rows)

    def to_core(k, w):
        return remote(mine.at[k, w, seg(1 - core)], cbuf.at[k, w], sc.at[k, w], rc.at[k, w], beside)

    def to_x(k):
        return remote(mine.at[k, 0, seg(core)], xbuf.at[k], sx.at[k], rx.at[k], opposite)

    def store(k):
        return pltpu.make_async_copy(
            cross.at[k % 2], cross_out.at[:, pl.ds(k * width, width)], so.at[k])

    def to_half(k):
        return remote(term.at[k, 1 - core], hbuf.at[k], sh.at[k], rh.at[k], beside)

    def to_piece(k, o):
        other, device = chip(o)
        return remote(sbuf.at[k, other], pbuf.at[k, me], sq.at[k, o], rq.at[k, me], device)

    def to_all(k, o):
        _, device = chip(o)
        ref = gbuf.at[k, core, me]
        return remote(ref, ref, sg.at[k, o], rg.at[k, me], device)

    def to_pair(k):
        ref = gbuf.at[k, core]
        return remote(ref, ref, sf.at[k], rf.at[k], beside)

    def half_sum(k):
        to_core(k, 0).wait_recv()

        def add(i, carry):
            at = pl.ds(pl.multiple_of(i * rows, rows), rows)
            own = pl.ds(pl.multiple_of(core * seg_rows + i * rows, rows), rows)
            total = mine[k, 0, own].astype(jnp.float32) + cbuf[k, 0, at].astype(jnp.float32)
            mine[k, 0, own] = total.astype(jnp.bfloat16)
            return carry

        lax.fori_loop(0, parts, add, 0)
        to_x(k).start()

    def own_sum(k):
        to_core(k, 1).wait_recv()
        to_x(k).wait_recv()
        if k >= 2:
            store(k - 2).wait()
        term[k] = jnp.zeros(term.shape[1:], jnp.float32)

        def add(i, carry):
            at = pl.ds(pl.multiple_of(i * rows, rows), rows)
            own = pl.ds(pl.multiple_of(core * seg_rows + i * rows, rows), rows)
            total = mine[k, 1, own].astype(jnp.float32) + cbuf[k, 1, at].astype(jnp.float32)
            total = -((total + xbuf[k, at].astype(jnp.float32)) * listed[at, k:k + 1])
            cross[k % 2, at] = total
            high = total.astype(jnp.bfloat16)
            low = (total - high.astype(jnp.float32)).astype(jnp.bfloat16)
            left = turned[k * width:(k + 1) * width, at]
            both = jnp.dot(left, high, preferred_element_type=jnp.float32)
            both += jnp.dot(left, low, preferred_element_type=jnp.float32)
            term[k] += both.reshape(2, half, width)
            return carry

        lax.fori_loop(0, parts, add, 0)
        to_half(k).start()
        store(k).start()

    def deal(k):
        to_half(k).wait_recv()
        sbuf[k] = (term[k, core] + hbuf[k]).reshape(chips, piece, width)
        for o in range(1, chips):
            to_piece(k, o).start()

    def collect(k):
        total = sbuf[k, me]
        for o in range(1, chips):
            other, device = chip(o)
            part = pbuf.at[k, other]
            remote(part, part, sq.at[k, o], rq.at[k, other], device).wait_recv()
            total = total + pbuf[k, other]
        gbuf[k, core, me] = total.astype(jnp.bfloat16)
        for o in range(1, chips):
            to_all(k, o).start()

    def pair(k):
        for o in range(1, chips):
            other, device = chip(o)
            ref = gbuf.at[k, core, other]
            remote(ref, ref, sg.at[k, o], rg.at[k, other], device).wait_recv()
        to_pair(k).start()

    def result(k):
        ref = gbuf.at[k, 1 - core]
        remote(ref, ref, sf.at[k], rf.at[k], beside).wait_recv()
        total = gbuf[k].astype(jnp.float32).reshape(width, width)
        diag_out[k] = diag_out[k] - total

    lax.fori_loop(0, steps + nz, step, 0)
    last = n_super - 1
    for k in range(n_super):
        complete(k * cap, (k + 1) * cap)
        products(k, 0, 0, per_side)
        to_core(k, 0).start()
        products(k, 1, 0, per_side - 1)
        half_sum(k)
        products(k, 1, per_side - 1, per_side)
        to_core(k, 1).start()
        if 0 < k < last:
            own_sum(k - 1)
        if k == last:
            if k > 1:
                deal(k - 2)
            if k:
                own_sum(k - 1)
                deal(k - 1)
            if k > 1:
                collect(k - 2)
    own_sum(last)
    deal(last)
    if last:
        collect(last - 1)
    given.wait()
    for k in range(last):
        pair(k)
    collect(last)
    for k in range(last):
        result(k)
    pair(last)
    result(last)

    def sent(t, carry):
        def size(g):
            return lane.at[g, one(t)]

        for o in range(1, ny):
            for l in range(nc):
                across(l, o, t).wait_send()
        for g in range(nz):
            @pl.when(jnp.logical_and(g <= z, z < nz - 1))
            def _():
                remote(size(g), size(g), su.at[g, t], rz.at[g, t], beside).wait_send()

            @pl.when(jnp.logical_and(g >= z, z > 0))
            def _():
                remote(size(g), size(g), sd.at[g, t], rz.at[g, t], beside).wait_send()

            @pl.when(g != c)
            def _():
                remote(size(g), size(g), sp.at[g, t], rz.at[g, t], beside).wait_send()
        return carry

    lax.fori_loop(0, steps, sent, 0)
    for k in range(n_super):
        for w in range(2):
            to_core(k, w).wait_send()
        to_x(k).wait_send()
        if k >= n_super - 2:
            store(k).wait()
        to_half(k).wait_send()
        for o in range(1, chips):
            to_piece(k, o).wait_send()
            to_all(k, o).wait_send()
        to_pair(k).wait_send()


def squeeze(member, first, blocks, cap):
    flags = lax.dynamic_slice_in_dim(member, first, blocks, 0).T.astype(jnp.int32)
    where = jnp.arange(blocks)
    rank = jnp.sum(jnp.where(where[None, :] < where[:, None], flags[:, None, :], 0), axis=2)
    hit = jnp.logical_and(rank[:, None, :] == jnp.arange(cap)[None, :, None], flags[:, None, :] > 0)
    return jnp.sum(jnp.where(hit, where, 0), axis=2), jnp.any(hit, axis=2)


def compact(cap, collective_id, ny, member, listed, panel_blocks, pivot_inverse,
            diagonal_inverse, inverse_tiles):
    n_super, width = pivot_inverse.shape[0], pivot_inverse.shape[1]
    seg_rows = panel_blocks.shape[0]
    nr, nc = lax.axis_size("prow"), lax.axis_size("pcol")
    nz, lanes = nr // ny, ny * nc
    sub = math.gcd(seg_rows, width)
    per, thin, halves = seg_rows // sub * n_super, sub // lanes, width // sub
    col_blocks = inverse_tiles.shape[1] // width
    bf16, f32 = jnp.bfloat16, jnp.float32
    smem = pl.BlockSpec(memory_space=pltpu.SMEM)
    vmem, hbm = pl.BlockSpec(memory_space=pltpu.VMEM), pl.BlockSpec(memory_space=pltpu.HBM)

    slots = n_super * cap
    z = lax.axis_index("prow") // ny
    block, full = squeeze(member, z * col_blocks, col_blocks, cap)
    source = block * (halves * n_super) + jnp.arange(n_super)[:, None]
    source = jnp.where(full, source, lanes * per).astype(jnp.int32).reshape(-1)
    packed, turned = pl.pallas_call(
        functools.partial(deal_kernel, nz, ny, nc, n_super),
        out_shape=(
            jax.ShapeDtypeStruct((slots, halves, thin, width), bf16),
            jax.ShapeDtypeStruct((n_super * width, seg_rows), bf16),
        ),
        in_specs=[smem, vmem, vmem, vmem],
        out_specs=(vmem, vmem),
        scratch_shapes=[
            pltpu.VMEM((lanes, per, thin, width), bf16),
            pltpu.VMEM((lanes * per + halves * n_super, thin, width), bf16),
            pltpu.VMEM((seg_rows, n_super * width), bf16),
        ] + [pltpu.SemaphoreType.DMA((per // n_super, lanes))] * 2,
        compiler_params=pltpu.CompilerParams(
            collective_id=collective_id, has_side_effects=True, vmem_limit_bytes=40 * 2**20,
        ),
        name="deal_listed",
    )(source, listed, panel_blocks, pivot_inverse)

    column, _ = squeeze(member, lax.axis_index("pcol") * col_blocks, col_blocks, cap)

    chips = nr * 2
    piece = width // 2 // chips
    depth = 2 if cap * 4 <= col_blocks * 3 else 1
    scratch = [((col_blocks, width, width), bf16)] * depth + [
        ((slots, halves, lanes, thin, width), bf16),
        ((n_super, 2, 2 * seg_rows, width), bf16), ((n_super, 2, seg_rows, width), bf16),
        ((n_super, seg_rows, width), bf16), ((2, seg_rows, width), f32),
        ((n_super, 2, width // 2, width), f32), ((n_super, width // 2, width), f32),
        ((n_super, chips, piece, width), f32), ((n_super, chips, piece, width), f32),
        ((n_super, 2, chips, piece, width), bf16),
    ]
    flow, one, two, many = (nz, slots), (n_super,), (n_super, 2), (n_super, chips)
    sems = [flow, flow, flow, flow, (lanes, slots), (nc, max(ny - 1, 1), slots)]
    sems += [(depth, col_blocks), (1,), two, two, one, one, one, one, one, many, many, many, many, one, one]
    cross, diagonal, _ = pl.pallas_call(
        functools.partial(main_kernel, nr, ny, nc, n_super, cap, depth),
        out_shape=(
            jax.ShapeDtypeStruct((seg_rows, n_super * width), f32),
            jax.ShapeDtypeStruct((n_super, width, width), f32),
            jax.ShapeDtypeStruct((nz, slots, halves, thin, width), bf16),
        ),
        in_specs=[smem, vmem, vmem, hbm, hbm, hbm],
        out_specs=(hbm, vmem, hbm),
        scratch_shapes=[pltpu.VMEM(s, t) for s, t in scratch]
        + [pltpu.SemaphoreType.DMA(s) for s in sems],
        compiler_params=pltpu.CompilerParams(
            collective_id=collective_id + 1, has_side_effects=True, vmem_limit_bytes=62 * 2**20,
        ),
        name="flow_multiply_sum",
    )(column.astype(jnp.int32).reshape(-1), listed, turned, packed, diagonal_inverse, inverse_tiles)
    return cross, diagonal


def on_device(inverse_tiles, panel_blocks, pivot_inverse, diagonal_inverse, ancestors):
    nr, nc = lax.axis_size("prow"), lax.axis_size("pcol")
    n_super, width = pivot_inverse.shape[0], pivot_inverse.shape[1]
    seg_rows = panel_blocks.shape[0]
    ny = nr // nc
    lanes, chips = ny * nc, nr * 2
    sub = math.gcd(seg_rows, width)
    fits = (
        nr == lanes and nc == 4 and sub % (lanes * 16) == 0
        and nr * nc * seg_rows // width % (12 * nc) == 0 and seg_rows % 3 == 0
        and width % (chips * 32) == 0 and inverse_tiles.shape[0] == nc * seg_rows
        and inverse_tiles.shape[0] % width == 0 and inverse_tiles.shape[1] % width == 0
    )
    if not fits:
        return general(inverse_tiles, panel_blocks, pivot_inverse, diagonal_inverse, ancestors)
    blocks = nr * nc * seg_rows // width
    member = jnp.any(jnp.arange(blocks)[:, None, None] == ancestors[None, :, :], axis=2)

    segment = lax.axis_index("prow") * nc + lax.axis_index("pcol")
    block_ids = (segment * seg_rows + lax.iota(jnp.int32, seg_rows)) // width
    listed = jnp.any(block_ids[:, None, None] == ancestors[None, :, :], axis=2).astype(jnp.float32)
    deep = blocks // nc
    caps = [deep * n // 12 for n in (7, 8, 9, 12)]
    deepest = jnp.max(jnp.sum(member.reshape(nc, deep, n_super).astype(jnp.int32), axis=1))
    level = sum((deepest > cap).astype(jnp.int32) for cap in caps[:-1])
    branches = [functools.partial(compact, cap, 2 * i, ny) for i, cap in enumerate(caps)]
    return lax.switch(level, branches, member, listed, panel_blocks, pivot_inverse,
                      diagonal_inverse, inverse_tiles)


def solution(mesh):
    in_specs = (P("prow", "pcol"), P(("prow", "pcol"), None), P(), P(), P())
    out_specs = (P(("prow", "pcol"), None), P())
    return jax.shard_map(
        on_device, mesh=mesh, in_specs=in_specs, out_specs=out_specs, check_vma=False
    )
```

```python
import functools
import math

import jax
import jax.numpy as jnp
from jax import lax
from jax.experimental import pallas as pl
from jax.experimental.pallas import tpu as pltpu
from jax.sharding import PartitionSpec as P

MESH = pl.DeviceIdType.MESH


def reduce_rows(partial, seg_rows):
    devices = lax.axis_size("pcol")
    width = partial.shape[1]
    me = lax.axis_index("pcol")
    if devices & (devices - 1):
        return lax.psum_scatter(partial, "pcol", scatter_dimension=0, tiled=True)
    value = partial.reshape(devices, seg_rows, width)
    bit = 1
    while bit < devices:
        mine = (me // bit) % 2
        halves = value.reshape(value.shape[0] // 2, 2, seg_rows, width)
        keep = jnp.where(mine == 0, halves[:, 0], halves[:, 1])
        send = jnp.where(mine == 0, halves[:, 1], halves[:, 0]).astype(jnp.bfloat16)
        got = lax.ppermute(send, "pcol", [(d, d ^ bit) for d in range(devices)])
        value = keep + got.astype(jnp.float32)
        bit *= 2
    return value.reshape(seg_rows, width)


def sum_everywhere(terms):
    axes = ("prow", "pcol")
    devices = lax.axis_size("prow") * lax.axis_size("pcol")
    rows = terms.shape[0] * terms.shape[1]
    if devices & (devices - 1) or rows % devices:
        return lax.psum(terms, axes)
    me = lax.axis_index("prow") * lax.axis_size("pcol") + lax.axis_index("pcol")
    value = terms.reshape(rows, terms.shape[2])
    bits = []
    bit = 1
    while bit < devices:
        bits.append(bit)
        bit *= 2
    for bit in bits:
        low = (me // bit) % 2 == 0
        half = value.shape[0] // 2
        keep = jnp.where(low, value[:half], value[half:])
        send = jnp.where(low, value[half:], value[:half])
        value = keep + lax.ppermute(send, axes, [(d, d ^ bit) for d in range(devices)])
    value = value.astype(jnp.bfloat16)
    for bit in reversed(bits):
        low = (me // bit) % 2 == 0
        got = lax.ppermute(value, axes, [(d, d ^ bit) for d in range(devices)])
        value = jnp.concatenate(
            [jnp.where(low, value, got), jnp.where(low, got, value)], axis=0
        )
    return value.astype(jnp.float32).reshape(terms.shape)


def general(inverse_tiles, panel_blocks, pivot_inverse, diagonal_inverse, ancestors):
    seg_rows = panel_blocks.shape[0]
    n_super = pivot_inverse.shape[0]
    width = pivot_inverse.shape[1]
    row_devices = lax.axis_size("prow")
    col_devices = lax.axis_size("pcol")
    segment = lax.axis_index("prow") * col_devices + lax.axis_index("pcol")
    row_ids = segment * seg_rows + lax.iota(jnp.int32, seg_rows)
    block_ids = row_ids // width
    listed = jnp.any(block_ids[:, None, None] == ancestors[None, :, :], axis=2).astype(jnp.float32)
    route = []
    for s in range(row_devices * col_devices):
        route.append((s, (s % row_devices) * col_devices + s // row_devices))
    crosses, terms, panels, scaled = [], [], [], []
    for k in range(n_super):
        normed = jnp.dot(
            panel_blocks[:, k * width:(k + 1) * width], pivot_inverse[k],
            preferred_element_type=jnp.float32,
        )
        own = (normed * listed[:, k:k + 1]).astype(jnp.bfloat16)
        scaled.append(own)
        moved = lax.ppermute(own, ("prow", "pcol"), route)
        panels.append(lax.all_gather(moved, "prow", axis=0, tiled=True))
    for k in range(n_super):
        product = jnp.dot(inverse_tiles, panels[k], preferred_element_type=jnp.float32)
        cross = -(reduce_rows(product, seg_rows) * listed[:, k:k + 1])
        crosses.append(cross)
        terms.append(lax.dot_general(
            scaled[k].astype(jnp.float32), cross, (((0,), (0,)), ((), ())),
            precision=lax.Precision.HIGHEST,
        ))
    diagonal = diagonal_inverse - sum_everywhere(jnp.stack(terms))
    return (jnp.concatenate(crosses, axis=1), diagonal)


def remote(src, dst, send, recv, device):
    return pltpu.make_async_remote_copy(
        src_ref=src, dst_ref=dst, send_sem=send, recv_sem=recv,
        device_id=device, device_id_type=MESH,
    )


def deal_kernel(nz, ny, nc, n_super, place, listed, panel, pivot, packed, turned,
                own, dense, scaled, s1, r1):
    lanes = ny * nc
    per, thin, width = own.shape[1:]
    parts, sub = per // n_super, thin * lanes
    slots, halves = packed.shape[:2]
    p, c = lax.axis_index("prow"), lax.axis_index("pcol")
    z, y = p // ny, lax.rem(p, ny)
    e = y * nc + c

    def peer(o):
        other = lax.rem(e + o, lanes)
        return other, (z * ny + other // nc, lax.rem(other, nc))

    barrier = pltpu.get_barrier_semaphore()
    for o in range(1, lanes):
        pl.semaphore_signal(barrier, inc=1, device_id=peer(o)[1], device_id_type=MESH)

    def deal(b, o):
        other, device = peer(o)
        return remote(own.at[other, pl.ds(b * n_super, n_super)],
                      dense.at[pl.ds(e * per + b * n_super, n_super)],
                      s1.at[b, o], r1.at[b, e], device)

    def home(b):
        return pltpu.make_async_copy(own.at[e, pl.ds(b * n_super, n_super)],
                                     dense.at[pl.ds(e * per + b * n_super, n_super)], r1.at[b, e])

    for b in range(parts):
        rows = slice(b * sub, (b + 1) * sub)
        for k in range(n_super):
            cols = slice(k * width, (k + 1) * width)
            normed = jnp.dot(panel[rows, cols], pivot[k], preferred_element_type=jnp.float32)
            normed = (normed * listed[rows, k:k + 1]).astype(jnp.bfloat16)
            scaled[rows, cols] = normed
            own[:, b * n_super + k] = normed.reshape(lanes, thin, width)
        if b == 0:
            pl.semaphore_wait(barrier, lanes - 1)
        for o in range(1, lanes):
            deal(b, o).start()
        home(b).start()
    for b in range(parts):
        rows = slice(b * sub, (b + 1) * sub)
        for k in range(n_super):
            cols = slice(k * width, (k + 1) * width)
            turned[cols, rows] = scaled[rows, cols].astype(jnp.float32).T.astype(jnp.bfloat16)
    for b in range(parts):
        home(b).wait()
        for o in range(1, lanes):
            other, device = peer(o)
            part = dense.at[pl.ds(other * per + b * n_super, n_super)]
            remote(part, part, s1.at[b, o], r1.at[b, other], device).wait_recv()

    blank = dense.shape[0] - lanes * per
    dense[lanes * per:] = jnp.zeros((blank, thin, width), dense.dtype)

    def pack(s, carry):
        at = place[s]
        for h in range(halves):
            packed[s, h] = dense[at + h * n_super]
        return carry

    lax.fori_loop(0, slots, pack, 0)
    for b in range(parts):
        for o in range(1, lanes):
            deal(b, o).wait_send()


def main_kernel(nr, ny, nc, n_super, cap, depth, column, listed, turned, packed, diag, tiles,
                cross_out, diag_out, lane, *scratch):
    panels, scratch = scratch[:depth], scratch[depth:]
    main_body(nr, ny, nc, n_super, cap, column, listed, turned, packed, diag, tiles,
              cross_out, diag_out, lane, panels, *scratch)


def main_body(nr, ny, nc, n_super, cap, column, listed, turned, packed, diag, tiles,
              cross_out, diag_out, lane, panels,
              held, mine, cbuf, xbuf, cross, term, hbuf, sbuf, pbuf, gbuf,
              su, sd, rz, sp, ro, sy,
              sa, ld, sc, rc, sx, rx, so, sh, rh, sq, rq, sg, rg, sf, rf):
    nz, lanes = nr // ny, ny * nc
    steps = packed.shape[0]
    width = diag_out.shape[1]
    depth = len(panels)
    chips, piece = pbuf.shape[1], pbuf.shape[2]
    half = width // 2
    parts = 3
    seg_rows = cross.shape[1]
    rows = seg_rows // parts
    per_side = mine.shape[2] // width
    p, c = lax.axis_index("prow"), lax.axis_index("pcol")
    z, y = p // ny, lax.rem(p, ny)
    e = y * nc + c
    x, core = c // 2, lax.rem(c, 2)
    me = p * (nc // 2) + x
    beside = (p, x * 2 + 1 - core)
    opposite = (p, (1 - x) * 2 + core)

    def chip(o):
        other = lax.rem(me + o, chips)
        return other, (other // (nc // 2), lax.rem(other, nc // 2) * 2 + core)

    barrier = pltpu.get_barrier_semaphore()
    for o in range(1, chips):
        pl.semaphore_signal(barrier, inc=1, device_id=chip(o)[1], device_id_type=MESH)
    for i in range(nc // 2):
        pl.semaphore_signal(barrier, inc=1, device_id=(p, 2 * i + 1 - core), device_id_type=MESH)

    n_tiles = 2 * n_super * per_side

    class fetch:
        def __init__(self, t, q):
            side = jnp.where(lax.rem(t, 2 * per_side) < per_side, 1 - x, x)
            at = pl.multiple_of((side * per_side + lax.rem(t, per_side)) * width, width)
            self.copies = [
                pltpu.make_async_copy(
                    tiles.at[pl.ds(at, width), j * width:(j + 1) * width],
                    panels[q].at[j], sa.at[q, j])
                for j in range(panels[0].shape[0])
            ]

        def start(self):
            for copy in self.copies:
                copy.start()

        def wait(self):
            for copy in self.copies:
                copy.wait()

    given = pltpu.make_async_copy(diag, diag_out, ld.at[0])
    fetch(0, 0).start()
    given.start()
    pl.semaphore_wait(barrier, chips - 1 + nc // 2)

    def one(t):
        return pl.ds(t, 1)

    def spread(g, t, source):
        @pl.when(jnp.logical_and(g <= z, z < nz - 1))
        def _():
            remote(source, lane.at[g, one(t)], su.at[g, t], rz.at[g, t], (p + ny, c)).start()

        @pl.when(jnp.logical_and(g >= z, z > 0))
        def _():
            remote(source, lane.at[g, one(t)], sd.at[g, t], rz.at[g, t], (p - ny, c)).start()

        @pl.when(g != c)
        def _():
            remote(source, held.at[one(t), :, e], sp.at[g, t], ro.at[e, t], (p, g)).start()

        @pl.when(g == c)
        def _():
            pltpu.make_async_copy(source, held.at[one(t), :, e], sp.at[g, t]).start()

    def across(l, o, t):
        part = held.at[one(t), :, y * nc + l]
        return remote(part, part, sy.at[l, o - 1, t], ro.at[y * nc + l, t],
                      (z * ny + lax.rem(y + o, ny), c))

    def arrived(other, t):
        part = held.at[one(t), :, other]
        remote(part, part, sp.at[0, t], ro.at[other, t], beside).wait_recv()

    away = jnp.maximum(z - c, c - z)

    def step(tau, carry):
        @pl.when(tau < steps)
        def _():
            spread(z, tau, packed.at[one(tau)])

        for d in range(1, nz):
            t = tau - d
            live = jnp.logical_and(t >= 0, t < steps)
            for g, ok in ((z - d, z - d >= 0), (z + d, z + d < nz)):
                @pl.when(jnp.logical_and(live, ok))
                def _():
                    part = lane.at[g, one(t)]
                    remote(part, part, su.at[g, t], rz.at[g, t], beside).wait_recv()
                    spread(g, t, part)

        t = tau - 1 - away

        @pl.when(jnp.logical_and(t >= 0, t < steps))
        def _():
            for l in range(nc):
                @pl.when(l == c)
                def _():
                    part = held.at[one(t), :, e]
                    pltpu.make_async_copy(part, part, sp.at[c, t]).wait()

                @pl.when(l != c)
                def _():
                    arrived(y * nc + l, t)

                for o in range(1, ny):
                    across(l, o, t).start()
        return carry

    def complete(first, last):
        def wait(t, carry):
            for o in range(1, ny):
                for l in range(nc):
                    arrived(lax.rem(y + o, ny) * nc + l, t)
            return carry

        lax.fori_loop(first, last, wait, 0)

    early = 2 * per_side * (n_super - 1)
    if any(steps - early + 2 * per_side * k < (k + 1) * cap for k in range(n_super - 1)):
        early = 0
    before = steps + nz - early

    def products(k, w, begin, end):
        def tile(r, carry):
            t = (k * 2 + w) * per_side + r
            if early and k < n_super - 1:
                step(before + t, 0)

            def following(q):
                @pl.when(t + 1 < n_tiles)
                def _():
                    fetch(t + 1, q).start()

            def work(q):
                if depth > 1:
                    following((q + 1) % depth)
                fetch(t, q).wait()

                def columns(n, carry):
                    cols = pl.ds(pl.multiple_of(n * half, half), half)
                    total = None
                    for i in range(cap):
                        block = held[k * cap + i, :, :, :, cols].reshape(width, half)
                        now = jnp.dot(panels[q][column[k * cap + i]], block,
                                      preferred_element_type=jnp.float32)
                        total = now if total is None else total + now
                    at = pl.ds(pl.multiple_of(r * width, width), width)
                    mine[k, w, at, cols] = total.astype(mine.dtype)
                    return carry

                lax.fori_loop(0, 2, columns, 0)
                if depth == 1:
                    following(0)

            if depth == 1:
                work(0)
            else:
                for q in range(depth):
                    pl.when(lax.rem(t, depth) == q)(functools.partial(work, q))
            return carry

        lax.fori_loop(begin, end, tile, 0)

    def seg(which):
        return pl.ds(pl.multiple_of(which * seg_rows, seg_rows), seg_rows)

    def to_core(k, w):
        return remote(mine.at[k, w, seg(1 - core)], cbuf.at[k, w], sc.at[k, w], rc.at[k, w], beside)

    def to_x(k):
        return remote(mine.at[k, 0, seg(core)], xbuf.at[k], sx.at[k], rx.at[k], opposite)

    def store(k):
        return pltpu.make_async_copy(
            cross.at[k % 2], cross_out.at[:, pl.ds(k * width, width)], so.at[k])

    def to_half(k):
        return remote(term.at[k, 1 - core], hbuf.at[k], sh.at[k], rh.at[k], beside)

    def to_piece(k, o):
        other, device = chip(o)
        return remote(sbuf.at[k, other], pbuf.at[k, me], sq.at[k, o], rq.at[k, me], device)

    def to_all(k, o):
        _, device = chip(o)
        ref = gbuf.at[k, core, me]
        return remote(ref, ref, sg.at[k, o], rg.at[k, me], device)

    def to_pair(k):
        ref = gbuf.at[k, core]
        return remote(ref, ref, sf.at[k], rf.at[k], beside)

    def half_sum(k):
        to_core(k, 0).wait_recv()

        def add(i, carry):
            at = pl.ds(pl.multiple_of(i * rows, rows), rows)
            own = pl.ds(pl.multiple_of(core * seg_rows + i * rows, rows), rows)
            total = mine[k, 0, own].astype(jnp.float32) + cbuf[k, 0, at].astype(jnp.float32)
            mine[k, 0, own] = total.astype(jnp.bfloat16)
            return carry

        lax.fori_loop(0, parts, add, 0)
        to_x(k).start()

    def own_sum(k):
        to_core(k, 1).wait_recv()
        to_x(k).wait_recv()
        if k >= 2:
            store(k - 2).wait()
        term[k] = jnp.zeros(term.shape[1:], jnp.float32)

        def add(i, carry):
            at = pl.ds(pl.multiple_of(i * rows, rows), rows)
            own = pl.ds(pl.multiple_of(core * seg_rows + i * rows, rows), rows)
            total = mine[k, 1, own].astype(jnp.float32) + cbuf[k, 1, at].astype(jnp.float32)
            total = -((total + xbuf[k, at].astype(jnp.float32)) * listed[at, k:k + 1])
            cross[k % 2, at] = total
            high = total.astype(jnp.bfloat16)
            low = (total - high.astype(jnp.float32)).astype(jnp.bfloat16)
            left = turned[k * width:(k + 1) * width, at]
            both = jnp.dot(left, high, preferred_element_type=jnp.float32)
            both += jnp.dot(left, low, preferred_element_type=jnp.float32)
            term[k] += both.reshape(2, half, width)
            return carry

        lax.fori_loop(0, parts, add, 0)
        to_half(k).start()
        store(k).start()

    def deal(k):
        to_half(k).wait_recv()
        sbuf[k] = (term[k, core] + hbuf[k]).reshape(chips, piece, width)
        for o in range(1, chips):
            to_piece(k, o).start()

    def collect(k):
        total = sbuf[k, me]
        for o in range(1, chips):
            other, device = chip(o)
            part = pbuf.at[k, other]
            remote(part, part, sq.at[k, o], rq.at[k, other], device).wait_recv()
            total = total + pbuf[k, other]
        gbuf[k, core, me] = total.astype(jnp.bfloat16)
        for o in range(1, chips):
            to_all(k, o).start()

    def pair(k):
        for o in range(1, chips):
            other, device = chip(o)
            ref = gbuf.at[k, core, other]
            remote(ref, ref, sg.at[k, o], rg.at[k, other], device).wait_recv()
        to_pair(k).start()

    def result(k):
        ref = gbuf.at[k, 1 - core]
        remote(ref, ref, sf.at[k], rf.at[k], beside).wait_recv()
        total = gbuf[k].astype(jnp.float32).reshape(width, width)
        diag_out[k] = diag_out[k] - total

    lax.fori_loop(0, before, step, 0)
    last = n_super - 1
    for k in range(n_super):
        complete(k * cap, (k + 1) * cap)
        products(k, 0, 0, per_side)
        to_core(k, 0).start()
        if k == last and k:
            deal(k - 1)
        if 0 < k < last:
            own_sum(k - 1)
        if k > 1:
            collect(k - 2)
        if k == last:
            products(k, 1, 0, per_side - 1)
            half_sum(k)
            products(k, 1, per_side - 1, per_side)
            to_core(k, 1).start()
        else:
            products(k, 1, 0, per_side)
            to_core(k, 1).start()
            half_sum(k)
            if k:
                deal(k - 1)
            if k == last - 1:
                own_sum(k)
    if last:
        collect(last - 1)
    own_sum(last)
    deal(last)
    given.wait()
    for k in range(last):
        pair(k)
    collect(last)
    for k in range(last):
        result(k)
    pair(last)
    result(last)

    def sent(t, carry):
        def size(g):
            return lane.at[g, one(t)]

        for o in range(1, ny):
            for l in range(nc):
                across(l, o, t).wait_send()
        for g in range(nz):
            @pl.when(jnp.logical_and(g <= z, z < nz - 1))
            def _():
                remote(size(g), size(g), su.at[g, t], rz.at[g, t], beside).wait_send()

            @pl.when(jnp.logical_and(g >= z, z > 0))
            def _():
                remote(size(g), size(g), sd.at[g, t], rz.at[g, t], beside).wait_send()

            @pl.when(g != c)
            def _():
                remote(size(g), size(g), sp.at[g, t], rz.at[g, t], beside).wait_send()
        return carry

    lax.fori_loop(0, steps, sent, 0)
    for k in range(n_super):
        for w in range(2):
            to_core(k, w).wait_send()
        to_x(k).wait_send()
        if k >= n_super - 2:
            store(k).wait()
        to_half(k).wait_send()
        for o in range(1, chips):
            to_piece(k, o).wait_send()
            to_all(k, o).wait_send()
        to_pair(k).wait_send()


def squeeze(member, first, blocks, cap):
    flags = lax.dynamic_slice_in_dim(member, first, blocks, 0).T.astype(jnp.int32)
    where = jnp.arange(blocks)
    rank = jnp.sum(jnp.where(where[None, :] < where[:, None], flags[:, None, :], 0), axis=2)
    hit = jnp.logical_and(rank[:, None, :] == jnp.arange(cap)[None, :, None], flags[:, None, :] > 0)
    return jnp.sum(jnp.where(hit, where, 0), axis=2), jnp.any(hit, axis=2)


def compact(cap, collective_id, ny, member, listed, panel_blocks, pivot_inverse,
            diagonal_inverse, inverse_tiles):
    n_super, width = pivot_inverse.shape[0], pivot_inverse.shape[1]
    seg_rows = panel_blocks.shape[0]
    nr, nc = lax.axis_size("prow"), lax.axis_size("pcol")
    nz, lanes = nr // ny, ny * nc
    sub = math.gcd(seg_rows, width)
    per, thin, halves = seg_rows // sub * n_super, sub // lanes, width // sub
    col_blocks = inverse_tiles.shape[1] // width
    bf16, f32 = jnp.bfloat16, jnp.float32
    smem = pl.BlockSpec(memory_space=pltpu.SMEM)
    vmem, hbm = pl.BlockSpec(memory_space=pltpu.VMEM), pl.BlockSpec(memory_space=pltpu.HBM)

    slots = n_super * cap
    z = lax.axis_index("prow") // ny
    block, full = squeeze(member, z * col_blocks, col_blocks, cap)
    source = block * (halves * n_super) + jnp.arange(n_super)[:, None]
    source = jnp.where(full, source, lanes * per).astype(jnp.int32).reshape(-1)
    packed, turned = pl.pallas_call(
        functools.partial(deal_kernel, nz, ny, nc, n_super),
        out_shape=(
            jax.ShapeDtypeStruct((slots, halves, thin, width), bf16),
            jax.ShapeDtypeStruct((n_super * width, seg_rows), bf16),
        ),
        in_specs=[smem, vmem, vmem, vmem],
        out_specs=(vmem, vmem),
        scratch_shapes=[
            pltpu.VMEM((lanes, per, thin, width), bf16),
            pltpu.VMEM((lanes * per + halves * n_super, thin, width), bf16),
            pltpu.VMEM((seg_rows, n_super * width), bf16),
        ] + [pltpu.SemaphoreType.DMA((per // n_super, lanes))] * 2,
        compiler_params=pltpu.CompilerParams(
            collective_id=collective_id, has_side_effects=True, vmem_limit_bytes=40 * 2**20,
        ),
        name="deal_listed",
    )(source, listed, panel_blocks, pivot_inverse)

    column, _ = squeeze(member, lax.axis_index("pcol") * col_blocks, col_blocks, cap)

    chips = nr * 2
    piece = width // 2 // chips
    depth = 2 if cap * 4 <= col_blocks * 3 else 1
    scratch = [((col_blocks, width, width), bf16)] * depth + [
        ((slots, halves, lanes, thin, width), bf16),
        ((n_super, 2, 2 * seg_rows, width), bf16), ((n_super, 2, seg_rows, width), bf16),
        ((n_super, seg_rows, width), bf16), ((2, seg_rows, width), f32),
        ((n_super, 2, width // 2, width), f32), ((n_super, width // 2, width), f32),
        ((n_super, chips, piece, width), f32), ((n_super, chips, piece, width), f32),
        ((n_super, 2, chips, piece, width), bf16),
    ]
    flow, one, two, many = (nz, slots), (n_super,), (n_super, 2), (n_super, chips)
    sems = [flow, flow, flow, flow, (lanes, slots), (nc, max(ny - 1, 1), slots)]
    sems += [(depth, col_blocks), (1,), two, two, one, one, one, one, one, many, many, many, many, one, one]
    cross, diagonal, _ = pl.pallas_call(
        functools.partial(main_kernel, nr, ny, nc, n_super, cap, depth),
        out_shape=(
            jax.ShapeDtypeStruct((seg_rows, n_super * width), f32),
            jax.ShapeDtypeStruct((n_super, width, width), f32),
            jax.ShapeDtypeStruct((nz, slots, halves, thin, width), bf16),
        ),
        in_specs=[smem, vmem, vmem, hbm, hbm, hbm],
        out_specs=(hbm, vmem, hbm),
        scratch_shapes=[pltpu.VMEM(s, t) for s, t in scratch]
        + [pltpu.SemaphoreType.DMA(s) for s in sems],
        compiler_params=pltpu.CompilerParams(
            collective_id=collective_id + 1, has_side_effects=True, vmem_limit_bytes=62 * 2**20,
        ),
        name="flow_multiply_sum",
    )(column.astype(jnp.int32).reshape(-1), listed, turned, packed, diagonal_inverse, inverse_tiles)
    return cross, diagonal


def on_device(inverse_tiles, panel_blocks, pivot_inverse, diagonal_inverse, ancestors):
    nr, nc = lax.axis_size("prow"), lax.axis_size("pcol")
    n_super, width = pivot_inverse.shape[0], pivot_inverse.shape[1]
    seg_rows = panel_blocks.shape[0]
    ny = nr // nc
    lanes, chips = ny * nc, nr * 2
    sub = math.gcd(seg_rows, width)
    fits = (
        nr == lanes and nc == 4 and sub % (lanes * 16) == 0
        and nr * nc * seg_rows // width % (12 * nc) == 0
        and seg_rows % 3 == 0
        and width % (chips * 32) == 0 and inverse_tiles.shape[0] == nc * seg_rows
        and inverse_tiles.shape[0] % width == 0 and inverse_tiles.shape[1] % width == 0
    )
    if not fits:
        return general(inverse_tiles, panel_blocks, pivot_inverse, diagonal_inverse, ancestors)
    blocks = nr * nc * seg_rows // width
    member = jnp.any(jnp.arange(blocks)[:, None, None] == ancestors[None, :, :], axis=2)

    segment = lax.axis_index("prow") * nc + lax.axis_index("pcol")
    block_ids = (segment * seg_rows + lax.iota(jnp.int32, seg_rows)) // width
    listed = jnp.any(block_ids[:, None, None] == ancestors[None, :, :], axis=2).astype(jnp.float32)
    deep = blocks // nc
    caps = [deep * n // 12 for n in (8, 9, 12)]
    deepest = jnp.max(jnp.sum(member.reshape(nc, deep, n_super).astype(jnp.int32), axis=1))
    level = sum((deepest > cap).astype(jnp.int32) for cap in caps[:-1])
    branches = [functools.partial(compact, cap, 2 * i, ny) for i, cap in enumerate(caps)]
    return lax.switch(level, branches, member, listed, panel_blocks, pivot_inverse,
                      diagonal_inverse, inverse_tiles)


def solution(mesh):
    in_specs = (P("prow", "pcol"), P(("prow", "pcol"), None), P(), P(), P())
    out_specs = (P(("prow", "pcol"), None), P())
    return jax.shard_map(
        on_device, mesh=mesh, in_specs=in_specs, out_specs=out_specs, check_vma=False
    )
```

```python
import functools
import math

import jax
import jax.numpy as jnp
from jax import lax
from jax.experimental import pallas as pl
from jax.experimental.pallas import tpu as pltpu
from jax.sharding import PartitionSpec as P

MESH = pl.DeviceIdType.MESH


def reduce_rows(partial, seg_rows):
    devices = lax.axis_size("pcol")
    width = partial.shape[1]
    me = lax.axis_index("pcol")
    if devices & (devices - 1):
        return lax.psum_scatter(partial, "pcol", scatter_dimension=0, tiled=True)
    value = partial.reshape(devices, seg_rows, width)
    bit = 1
    while bit < devices:
        mine = (me // bit) % 2
        halves = value.reshape(value.shape[0] // 2, 2, seg_rows, width)
        keep = jnp.where(mine == 0, halves[:, 0], halves[:, 1])
        send = jnp.where(mine == 0, halves[:, 1], halves[:, 0]).astype(jnp.bfloat16)
        got = lax.ppermute(send, "pcol", [(d, d ^ bit) for d in range(devices)])
        value = keep + got.astype(jnp.float32)
        bit *= 2
    return value.reshape(seg_rows, width)


def sum_everywhere(terms):
    axes = ("prow", "pcol")
    devices = lax.axis_size("prow") * lax.axis_size("pcol")
    rows = terms.shape[0] * terms.shape[1]
    if devices & (devices - 1) or rows % devices:
        return lax.psum(terms, axes)
    me = lax.axis_index("prow") * lax.axis_size("pcol") + lax.axis_index("pcol")
    value = terms.reshape(rows, terms.shape[2])
    bits = []
    bit = 1
    while bit < devices:
        bits.append(bit)
        bit *= 2
    for bit in bits:
        low = (me // bit) % 2 == 0
        half = value.shape[0] // 2
        keep = jnp.where(low, value[:half], value[half:])
        send = jnp.where(low, value[half:], value[:half])
        value = keep + lax.ppermute(send, axes, [(d, d ^ bit) for d in range(devices)])
    value = value.astype(jnp.bfloat16)
    for bit in reversed(bits):
        low = (me // bit) % 2 == 0
        got = lax.ppermute(value, axes, [(d, d ^ bit) for d in range(devices)])
        value = jnp.concatenate(
            [jnp.where(low, value, got), jnp.where(low, got, value)], axis=0
        )
    return value.astype(jnp.float32).reshape(terms.shape)


def general(inverse_tiles, panel_blocks, pivot_inverse, diagonal_inverse, ancestors):
    seg_rows = panel_blocks.shape[0]
    n_super = pivot_inverse.shape[0]
    width = pivot_inverse.shape[1]
    row_devices = lax.axis_size("prow")
    col_devices = lax.axis_size("pcol")
    segment = lax.axis_index("prow") * col_devices + lax.axis_index("pcol")
    row_ids = segment * seg_rows + lax.iota(jnp.int32, seg_rows)
    block_ids = row_ids // width
    listed = jnp.any(block_ids[:, None, None] == ancestors[None, :, :], axis=2).astype(jnp.float32)
    route = []
    for s in range(row_devices * col_devices):
        route.append((s, (s % row_devices) * col_devices + s // row_devices))
    crosses, terms, panels, scaled = [], [], [], []
    for k in range(n_super):
        normed = jnp.dot(
            panel_blocks[:, k * width:(k + 1) * width], pivot_inverse[k],
            preferred_element_type=jnp.float32,
        )
        own = (normed * listed[:, k:k + 1]).astype(jnp.bfloat16)
        scaled.append(own)
        moved = lax.ppermute(own, ("prow", "pcol"), route)
        panels.append(lax.all_gather(moved, "prow", axis=0, tiled=True))
    for k in range(n_super):
        product = jnp.dot(inverse_tiles, panels[k], preferred_element_type=jnp.float32)
        cross = -(reduce_rows(product, seg_rows) * listed[:, k:k + 1])
        crosses.append(cross)
        terms.append(lax.dot_general(
            scaled[k].astype(jnp.float32), cross, (((0,), (0,)), ((), ())),
            precision=lax.Precision.HIGHEST,
        ))
    diagonal = diagonal_inverse - sum_everywhere(jnp.stack(terms))
    return (jnp.concatenate(crosses, axis=1), diagonal)


def remote(src, dst, send, recv, device):
    return pltpu.make_async_remote_copy(
        src_ref=src, dst_ref=dst, send_sem=send, recv_sem=recv,
        device_id=device, device_id_type=MESH,
    )


def deal_kernel(nz, ny, nc, n_super, place, listed, panel, pivot, packed_out, turned_out,
                packed, turned, own, dense, scaled, s1, r1, so):
    lanes = ny * nc
    per, thin, width = own.shape[1:]
    parts, sub = per // n_super, thin * lanes
    slots, halves = packed.shape[:2]
    p, c = lax.axis_index("prow"), lax.axis_index("pcol")
    z, y = p // ny, lax.rem(p, ny)
    e = y * nc + c

    def peer(o):
        other = lax.rem(e + o, lanes)
        return other, (z * ny + other // nc, lax.rem(other, nc))

    barrier = pltpu.get_barrier_semaphore()
    for o in range(1, lanes):
        pl.semaphore_signal(barrier, inc=1, device_id=peer(o)[1], device_id_type=MESH)

    def deal(b, o):
        other, device = peer(o)
        return remote(own.at[other, pl.ds(b * n_super, n_super)],
                      dense.at[pl.ds(e * per + b * n_super, n_super)],
                      s1.at[b, o], r1.at[b, e], device)

    def home(b):
        return pltpu.make_async_copy(own.at[e, pl.ds(b * n_super, n_super)],
                                     dense.at[pl.ds(e * per + b * n_super, n_super)], r1.at[b, e])

    for b in range(parts):
        rows = slice(b * sub, (b + 1) * sub)
        for k in range(n_super):
            cols = slice(k * width, (k + 1) * width)
            normed = jnp.dot(panel[rows, cols], pivot[k], preferred_element_type=jnp.float32)
            normed = (normed * listed[rows, k:k + 1]).astype(jnp.bfloat16)
            scaled[rows, cols] = normed
            own[:, b * n_super + k] = normed.reshape(lanes, thin, width)
        if b == 0:
            pl.semaphore_wait(barrier, lanes - 1)
        for o in range(1, lanes):
            deal(b, o).start()
        home(b).start()
    for b in range(parts):
        rows = slice(b * sub, (b + 1) * sub)
        for k in range(n_super):
            cols = slice(k * width, (k + 1) * width)
            turned[cols, rows] = scaled[rows, cols].astype(jnp.float32).T.astype(jnp.bfloat16)
    store_turned = pltpu.make_async_copy(turned, turned_out, so.at[0])
    store_turned.start()
    for b in range(parts):
        home(b).wait()
        for o in range(1, lanes):
            other, device = peer(o)
            part = dense.at[pl.ds(other * per + b * n_super, n_super)]
            remote(part, part, s1.at[b, o], r1.at[b, other], device).wait_recv()

    blank = dense.shape[0] - lanes * per
    dense[lanes * per:] = jnp.zeros((blank, thin, width), dense.dtype)

    def pack(s, carry):
        at = place[s]
        for h in range(halves):
            packed[s, h] = dense[at + h * n_super]
        return carry

    lax.fori_loop(0, slots, pack, 0)
    store_packed = pltpu.make_async_copy(packed, packed_out, so.at[1])
    store_packed.start()
    for b in range(parts):
        for o in range(1, lanes):
            deal(b, o).wait_send()
    store_turned.wait()
    store_packed.wait()


def main_kernel(nr, ny, nc, n_super, cap, depth, column, listed, turned_in, packed, diag, tiles,
                cross_out, diag_out, lane, *scratch):
    panels, scratch = scratch[:depth], scratch[depth:]
    main_body(nr, ny, nc, n_super, cap, column, listed, turned_in, packed, diag, tiles,
              cross_out, diag_out, lane, panels, *scratch)


def main_body(nr, ny, nc, n_super, cap, column, listed, turned_in, packed, diag, tiles,
              cross_out, diag_out, lane, panels,
              turned, held, mine, cbuf, xbuf, cross, term, hbuf, sbuf, pbuf, gbuf,
              su, sd, rz, sp, ro, sy,
              sa, ld, sc, rc, sx, rx, so, sh, rh, sq, rq, sg, rg, sf, rf):
    nz, lanes = nr // ny, ny * nc
    steps = packed.shape[0]
    width = diag_out.shape[1]
    depth = len(panels)
    chips, piece = pbuf.shape[1], pbuf.shape[2]
    half = width // 2
    parts = 3
    seg_rows = cross.shape[1]
    rows = seg_rows // parts
    per_side = mine.shape[2] // width
    p, c = lax.axis_index("prow"), lax.axis_index("pcol")
    z, y = p // ny, lax.rem(p, ny)
    e = y * nc + c
    x, core = c // 2, lax.rem(c, 2)
    me = p * (nc // 2) + x
    beside = (p, x * 2 + 1 - core)
    opposite = (p, (1 - x) * 2 + core)

    def chip(o):
        other = lax.rem(me + o, chips)
        return other, (other // (nc // 2), lax.rem(other, nc // 2) * 2 + core)

    barrier = pltpu.get_barrier_semaphore()
    for o in range(1, chips):
        pl.semaphore_signal(barrier, inc=1, device_id=chip(o)[1], device_id_type=MESH)
    for i in range(nc // 2):
        pl.semaphore_signal(barrier, inc=1, device_id=(p, 2 * i + 1 - core), device_id_type=MESH)

    n_tiles = 2 * n_super * per_side

    class fetch:
        def __init__(self, t, q):
            side = jnp.where(lax.rem(t, 2 * per_side) < per_side, 1 - x, x)
            at = pl.multiple_of((side * per_side + lax.rem(t, per_side)) * width, width)
            self.copies = [
                pltpu.make_async_copy(
                    tiles.at[pl.ds(at, width), j * width:(j + 1) * width],
                    panels[q].at[j], sa.at[q, j])
                for j in range(panels[0].shape[0])
            ]

        def start(self):
            for copy in self.copies:
                copy.start()

        def wait(self):
            for copy in self.copies:
                copy.wait()

    given = pltpu.make_async_copy(diag, diag_out, ld.at[0])
    fetch(0, 0).start()
    given.start()
    turning = pltpu.make_async_copy(turned_in, turned, ld.at[1])
    turning.start()
    pl.semaphore_wait(barrier, chips - 1 + nc // 2)

    def one(t):
        return pl.ds(t, 1)

    def spread(g, t, source):
        @pl.when(jnp.logical_and(g <= z, z < nz - 1))
        def _():
            remote(source, lane.at[g, one(t)], su.at[g, t], rz.at[g, t], (p + ny, c)).start()

        @pl.when(jnp.logical_and(g >= z, z > 0))
        def _():
            remote(source, lane.at[g, one(t)], sd.at[g, t], rz.at[g, t], (p - ny, c)).start()

        @pl.when(g != c)
        def _():
            remote(source, held.at[one(t), :, e], sp.at[g, t], ro.at[e, t], (p, g)).start()

        @pl.when(g == c)
        def _():
            pltpu.make_async_copy(source, held.at[one(t), :, e], sp.at[g, t]).start()

    def across(l, o, t):
        part = held.at[one(t), :, y * nc + l]
        return remote(part, part, sy.at[l, o - 1, t], ro.at[y * nc + l, t],
                      (z * ny + lax.rem(y + o, ny), c))

    def arrived(other, t):
        part = held.at[one(t), :, other]
        remote(part, part, sp.at[0, t], ro.at[other, t], beside).wait_recv()

    away = jnp.maximum(z - c, c - z)

    def step(tau, carry):
        @pl.when(tau < steps)
        def _():
            spread(z, tau, packed.at[one(tau)])

        for d in range(1, nz):
            t = tau - d
            live = jnp.logical_and(t >= 0, t < steps)
            for g, ok in ((z - d, z - d >= 0), (z + d, z + d < nz)):
                @pl.when(jnp.logical_and(live, ok))
                def _():
                    part = lane.at[g, one(t)]
                    remote(part, part, su.at[g, t], rz.at[g, t], beside).wait_recv()
                    spread(g, t, part)

        t = tau - 1 - away

        @pl.when(jnp.logical_and(t >= 0, t < steps))
        def _():
            for l in range(nc):
                @pl.when(l == c)
                def _():
                    part = held.at[one(t), :, e]
                    pltpu.make_async_copy(part, part, sp.at[c, t]).wait()

                @pl.when(l != c)
                def _():
                    arrived(y * nc + l, t)

                for o in range(1, ny):
                    across(l, o, t).start()
        return carry

    def complete(first, last):
        def wait(t, carry):
            for o in range(1, ny):
                for l in range(nc):
                    arrived(lax.rem(y + o, ny) * nc + l, t)
            return carry

        lax.fori_loop(first, last, wait, 0)

    early = 2 * per_side * (n_super - 1)
    if any(steps - early + 2 * per_side * k < (k + 1) * cap for k in range(n_super - 1)):
        early = 0
    before = steps + nz - early

    def products(between):
        def tile(t, carry):
            k, w = lax.div(t, 2 * per_side), lax.rem(lax.div(t, per_side), 2)
            r = lax.rem(t, per_side)

            @pl.when(lax.rem(t, 2 * per_side) == 0)
            def _():
                complete(k * cap, (k + 1) * cap)

            if early:
                @pl.when(t < early)
                def _():
                    step(before + t, 0)

            def following(q):
                @pl.when(t + 1 < n_tiles)
                def _():
                    fetch(t + 1, q).start()

            def work(q):
                if depth > 1:
                    following((q + 1) % depth)
                fetch(t, q).wait()

                def columns(n, carry):
                    cols = pl.ds(pl.multiple_of(n * half, half), half)
                    total = None
                    for i in range(cap):
                        block = held[k * cap + i, :, :, :, cols].reshape(width, half)
                        now = jnp.dot(panels[q][column[k * cap + i]], block,
                                      preferred_element_type=jnp.float32)
                        total = now if total is None else total + now
                    at = pl.ds(pl.multiple_of(r * width, width), width)
                    mine[k, w, at, cols] = total.astype(mine.dtype)
                    return carry

                lax.fori_loop(0, 2, columns, 0)
                if depth == 1:
                    following(0)

            if depth == 1:
                work(0)
            else:
                for q in range(depth):
                    pl.when(lax.rem(t, depth) == q)(functools.partial(work, q))

            @pl.when(r == per_side - 1)
            def _():
                to_core(k, w).start()

            for after, calls in between.items():
                @pl.when(t == after)
                def _():
                    for call, which in calls:
                        call(which)
            return carry

        lax.fori_loop(0, n_tiles, tile, 0)

    def seg(which):
        return pl.ds(pl.multiple_of(which * seg_rows, seg_rows), seg_rows)

    def to_core(k, w):
        return remote(mine.at[k, w, seg(1 - core)], cbuf.at[k, w], sc.at[k, w], rc.at[k, w], beside)

    def to_x(k):
        return remote(mine.at[k, 0, seg(core)], xbuf.at[k], sx.at[k], rx.at[k], opposite)

    def store(k):
        return pltpu.make_async_copy(
            cross.at[k % 2], cross_out.at[:, pl.ds(k * width, width)], so.at[k])

    def to_half(k):
        return remote(term.at[k, 1 - core], hbuf.at[k], sh.at[k], rh.at[k], beside)

    def to_piece(k, o):
        other, device = chip(o)
        return remote(sbuf.at[k, other], pbuf.at[k, me], sq.at[k, o], rq.at[k, me], device)

    def to_all(k, o):
        _, device = chip(o)
        ref = gbuf.at[k, core, me]
        return remote(ref, ref, sg.at[k, o], rg.at[k, me], device)

    def to_pair(k):
        ref = gbuf.at[k, core]
        return remote(ref, ref, sf.at[k], rf.at[k], beside)

    def half_sum(k):
        to_core(k, 0).wait_recv()

        def add(i, carry):
            at = pl.ds(pl.multiple_of(i * rows, rows), rows)
            own = pl.ds(pl.multiple_of(core * seg_rows + i * rows, rows), rows)
            total = mine[k, 0, own].astype(jnp.float32) + cbuf[k, 0, at].astype(jnp.float32)
            mine[k, 0, own] = total.astype(jnp.bfloat16)
            return carry

        lax.fori_loop(0, parts, add, 0)
        to_x(k).start()

    def own_sum(k):
        to_core(k, 1).wait_recv()
        to_x(k).wait_recv()
        if k >= 2:
            store(k - 2).wait()
        term[k] = jnp.zeros(term.shape[1:], jnp.float32)
        if k == 0:
            turning.wait()

        def add(i, carry):
            at = pl.ds(pl.multiple_of(i * rows, rows), rows)
            own = pl.ds(pl.multiple_of(core * seg_rows + i * rows, rows), rows)
            total = mine[k, 1, own].astype(jnp.float32) + cbuf[k, 1, at].astype(jnp.float32)
            total = -((total + xbuf[k, at].astype(jnp.float32)) * listed[at, k:k + 1])
            cross[k % 2, at] = total
            high = total.astype(jnp.bfloat16)
            low = (total - high.astype(jnp.float32)).astype(jnp.bfloat16)
            left = turned[k * width:(k + 1) * width, at]
            both = jnp.dot(left, high, preferred_element_type=jnp.float32)
            both += jnp.dot(left, low, preferred_element_type=jnp.float32)
            term[k] += both.reshape(2, half, width)
            return carry

        lax.fori_loop(0, parts, add, 0)
        to_half(k).start()
        store(k).start()

    def deal(k):
        to_half(k).wait_recv()
        sbuf[k] = (term[k, core] + hbuf[k]).reshape(chips, piece, width)
        for o in range(1, chips):
            to_piece(k, o).start()

    def collect(k):
        total = sbuf[k, me]
        for o in range(1, chips):
            other, device = chip(o)
            part = pbuf.at[k, other]
            remote(part, part, sq.at[k, o], rq.at[k, other], device).wait_recv()
            total = total + pbuf[k, other]
        gbuf[k, core, me] = total.astype(jnp.bfloat16)
        for o in range(1, chips):
            to_all(k, o).start()

    def pair(k):
        for o in range(1, chips):
            other, device = chip(o)
            ref = gbuf.at[k, core, other]
            remote(ref, ref, sg.at[k, o], rg.at[k, other], device).wait_recv()
        to_pair(k).start()

    def result(k):
        ref = gbuf.at[k, 1 - core]
        remote(ref, ref, sf.at[k], rf.at[k], beside).wait_recv()
        total = gbuf[k].astype(jnp.float32).reshape(width, width)
        diag_out[k] = diag_out[k] - total

    lax.fori_loop(0, before, step, 0)
    last = n_super - 1
    between = {}
    for k in range(n_super):
        first = 2 * per_side * k
        middle, end = [], [] if k == last else [(half_sum, k)]
        if k == last and k:
            middle.append((deal, k - 1))
        if 0 < k < last:
            middle.append((own_sum, k - 1))
        if k > 1:
            middle.append((collect, k - 2))
        if k == last:
            between[first + 2 * per_side - 2] = [(half_sum, k)]
        if 0 < k < last:
            end.append((deal, k - 1))
        if k == last - 1:
            end.append((own_sum, k))
        between[first + per_side - 1] = middle
        between[first + 2 * per_side - 1] = end
    products({after: calls for after, calls in between.items() if calls})
    if last:
        collect(last - 1)
    own_sum(last)
    deal(last)
    given.wait()
    for k in range(last):
        pair(k)
    collect(last)
    for k in range(last):
        result(k)
    pair(last)
    result(last)

    def sent(t, carry):
        def size(g):
            return lane.at[g, one(t)]

        for o in range(1, ny):
            for l in range(nc):
                across(l, o, t).wait_send()
        for g in range(nz):
            @pl.when(jnp.logical_and(g <= z, z < nz - 1))
            def _():
                remote(size(g), size(g), su.at[g, t], rz.at[g, t], beside).wait_send()

            @pl.when(jnp.logical_and(g >= z, z > 0))
            def _():
                remote(size(g), size(g), sd.at[g, t], rz.at[g, t], beside).wait_send()

            @pl.when(g != c)
            def _():
                remote(size(g), size(g), sp.at[g, t], rz.at[g, t], beside).wait_send()
        return carry

    lax.fori_loop(0, steps, sent, 0)
    for k in range(n_super):
        for w in range(2):
            to_core(k, w).wait_send()
        to_x(k).wait_send()
        if k >= n_super - 2:
            store(k).wait()
        to_half(k).wait_send()
        for o in range(1, chips):
            to_piece(k, o).wait_send()
            to_all(k, o).wait_send()
        to_pair(k).wait_send()


def squeeze(member, first, blocks, cap):
    flags = lax.dynamic_slice_in_dim(member, first, blocks, 0).T.astype(jnp.int32)
    where = jnp.arange(blocks)
    rank = jnp.sum(jnp.where(where[None, :] < where[:, None], flags[:, None, :], 0), axis=2)
    hit = jnp.logical_and(rank[:, None, :] == jnp.arange(cap)[None, :, None], flags[:, None, :] > 0)
    return jnp.sum(jnp.where(hit, where, 0), axis=2), jnp.any(hit, axis=2)


def compact(cap, collective_id, ny, member, listed, panel_blocks, pivot_inverse,
            diagonal_inverse, inverse_tiles):
    n_super, width = pivot_inverse.shape[0], pivot_inverse.shape[1]
    seg_rows = panel_blocks.shape[0]
    nr, nc = lax.axis_size("prow"), lax.axis_size("pcol")
    nz, lanes = nr // ny, ny * nc
    sub = math.gcd(seg_rows, width)
    per, thin, halves = seg_rows // sub * n_super, sub // lanes, width // sub
    col_blocks = inverse_tiles.shape[1] // width
    bf16, f32 = jnp.bfloat16, jnp.float32
    smem = pl.BlockSpec(memory_space=pltpu.SMEM)
    vmem, hbm = pl.BlockSpec(memory_space=pltpu.VMEM), pl.BlockSpec(memory_space=pltpu.HBM)

    slots = n_super * cap
    z = lax.axis_index("prow") // ny
    block, full = squeeze(member, z * col_blocks, col_blocks, cap)
    source = block * (halves * n_super) + jnp.arange(n_super)[:, None]
    source = jnp.where(full, source, lanes * per).astype(jnp.int32).reshape(-1)
    packed, turned = pl.pallas_call(
        functools.partial(deal_kernel, nz, ny, nc, n_super),
        out_shape=(
            jax.ShapeDtypeStruct((slots, halves, thin, width), bf16),
            jax.ShapeDtypeStruct((n_super * width, seg_rows), bf16),
        ),
        in_specs=[smem, vmem, vmem, vmem],
        out_specs=(hbm, hbm),
        scratch_shapes=[
            pltpu.VMEM((slots, halves, thin, width), bf16),
            pltpu.VMEM((n_super * width, seg_rows), bf16),
            pltpu.VMEM((lanes, per, thin, width), bf16),
            pltpu.VMEM((lanes * per + halves * n_super, thin, width), bf16),
            pltpu.VMEM((seg_rows, n_super * width), bf16),
        ] + [pltpu.SemaphoreType.DMA((per // n_super, lanes))] * 2 + [
            pltpu.SemaphoreType.DMA((2,)),
        ],
        compiler_params=pltpu.CompilerParams(
            collective_id=collective_id, has_side_effects=True, vmem_limit_bytes=40 * 2**20,
        ),
        name="deal_listed",
    )(source, listed, panel_blocks, pivot_inverse)

    column, _ = squeeze(member, lax.axis_index("pcol") * col_blocks, col_blocks, cap)

    chips = nr * 2
    piece = width // 2 // chips
    depth = 2 if cap * 4 <= col_blocks * 3 else 1
    scratch = [((col_blocks, width, width), bf16)] * depth + [
        ((n_super * width, seg_rows), bf16),
        ((slots, halves, lanes, thin, width), bf16),
        ((n_super, 2, 2 * seg_rows, width), bf16), ((n_super, 2, seg_rows, width), bf16),
        ((n_super, seg_rows, width), bf16), ((2, seg_rows, width), f32),
        ((n_super, 2, width // 2, width), f32), ((n_super, width // 2, width), f32),
        ((n_super, chips, piece, width), f32), ((n_super, chips, piece, width), f32),
        ((n_super, 2, chips, piece, width), bf16),
    ]
    flow, one, two, many = (nz, slots), (n_super,), (n_super, 2), (n_super, chips)
    sems = [flow, flow, flow, flow, (lanes, slots), (nc, max(ny - 1, 1), slots)]
    sems += [(depth, col_blocks), (2,), two, two, one, one, one, one, one, many, many, many, many, one, one]
    cross, diagonal, _ = pl.pallas_call(
        functools.partial(main_kernel, nr, ny, nc, n_super, cap, depth),
        out_shape=(
            jax.ShapeDtypeStruct((seg_rows, n_super * width), f32),
            jax.ShapeDtypeStruct((n_super, width, width), f32),
            jax.ShapeDtypeStruct((nz, slots, halves, thin, width), bf16),
        ),
        in_specs=[smem, vmem, hbm, hbm, hbm, hbm],
        out_specs=(hbm, vmem, hbm),
        scratch_shapes=[pltpu.VMEM(s, t) for s, t in scratch]
        + [pltpu.SemaphoreType.DMA(s) for s in sems],
        compiler_params=pltpu.CompilerParams(
            collective_id=collective_id + 1, has_side_effects=True, vmem_limit_bytes=62 * 2**20,
        ),
        name="flow_multiply_sum",
    )(column.astype(jnp.int32).reshape(-1), listed, turned, packed, diagonal_inverse, inverse_tiles)
    return cross, diagonal


def on_device(inverse_tiles, panel_blocks, pivot_inverse, diagonal_inverse, ancestors):
    nr, nc = lax.axis_size("prow"), lax.axis_size("pcol")
    n_super, width = pivot_inverse.shape[0], pivot_inverse.shape[1]
    seg_rows = panel_blocks.shape[0]
    ny = nr // nc
    lanes, chips = ny * nc, nr * 2
    sub = math.gcd(seg_rows, width)
    fits = (
        nr == lanes and nc == 4 and sub % (lanes * 16) == 0
        and nr * nc * seg_rows // width % (12 * nc) == 0
        and seg_rows % 3 == 0
        and width % (chips * 32) == 0 and inverse_tiles.shape[0] == nc * seg_rows
        and inverse_tiles.shape[0] % width == 0 and inverse_tiles.shape[1] % width == 0
    )
    if not fits:
        return general(inverse_tiles, panel_blocks, pivot_inverse, diagonal_inverse, ancestors)
    blocks = nr * nc * seg_rows // width
    member = jnp.any(jnp.arange(blocks)[:, None, None] == ancestors[None, :, :], axis=2)

    segment = lax.axis_index("prow") * nc + lax.axis_index("pcol")
    block_ids = (segment * seg_rows + lax.iota(jnp.int32, seg_rows)) // width
    listed = jnp.any(block_ids[:, None, None] == ancestors[None, :, :], axis=2).astype(jnp.float32)
    deep = blocks // nc
    caps = [deep * n // 12 for n in (7, 8, 9, 12)]
    deepest = jnp.max(jnp.sum(member.reshape(nc, deep, n_super).astype(jnp.int32), axis=1))
    args = (member, listed, panel_blocks, pivot_inverse, diagonal_inverse, inverse_tiles)
    branches = [functools.partial(compact, cap, 2 * i, ny) for i, cap in enumerate(caps)]
    run = branches[-1]
    for cap, branch in reversed(list(zip(caps, branches))[:-1]):
        run = functools.partial(lax.cond, deepest <= cap, branch, run)
    return run(*args)


def solution(mesh):
    in_specs = (P("prow", "pcol"), P(("prow", "pcol"), None), P(), P(), P())
    out_specs = (P(("prow", "pcol"), None), P())
    return jax.shard_map(
        on_device, mesh=mesh, in_specs=in_specs, out_specs=out_specs, check_vma=False
    )
```
